32 devices in a mesh: half: 2 (over x), seq: 4 (over z), head: 4 (over y, core).
Axes of the slice: x: 2, y: 2, z: 4, core: 2. Of those that a mesh axis runs over, the one named last changes fastest.
Arguments:
- enc_states: bfloat16 [8192, 4096], P(('half', 'seq')), may hold values from -64 to 64
- norm_gain: float32 [4096], replicated, may hold values from 0.25 to 4
- kv_weight: bfloat16 [4096, 1024], P(None, 'head'), may hold values from -1 to 1
- queries: bfloat16 [1024, 4096], P(('half', 'seq'), 'head'), may hold values from -512 to 512
- cotangent: bfloat16 [1024, 4096], P(('half', 'seq'), 'head'), may hold values from -8 to 8
Outputs:
- context: bfloat16 [1024, 4096], P(('half', 'seq'), 'head')
- d_queries: bfloat16 [1024, 4096], P(('half', 'seq'), 'head')
- d_keys_values: bfloat16 [8192, 1024], P(('half', 'seq'), 'head')
The draws below stay inside these ranges and needn't reach their ends.
All inputs are finite; a program needn't handle non-finite values.
Results may differ from the reference program's by a relative error of at most 0.013.
The reference program's roundings to bfloat16 on the way count: a program that leaves them out, or rounds other values in their place, can miss the bound.
Values may be sent and summed in bfloat16 or wider, within the bound.
No kernel may reach another device: no remote copies, remote signals or barrier semaphores. Data moves between devices by JAX's collectives and lax.ppermute only.
A program may use at most 128 MiB of HBM per device.

```python
import jax
import jax.numpy as jnp
from jax import lax

D = 4096
H = 64
G = 8
HD = 64
ENC = 8192
DEC = 1024


def encoder_draws(key):
    state_key = jax.random.fold_in(key, 101)
    gain_key = jax.random.fold_in(key, 202)
    weight_key = jax.random.fold_in(key, 303)
    states = jnp.clip(jax.random.normal(state_key, (ENC, D), jnp.float32), -6.0, 6.0)
    gains = jax.random.uniform(gain_key, (D,), jnp.float32, 0.5, 1.5)
    weight = jnp.clip(jax.random.normal(weight_key, (D, 2 * G * HD), jnp.float32) / jnp.sqrt(1.0 * D), -1.0, 1.0)
    return (states, gains, weight)


def draw_enc_states(key, part):
    states, gains, weight = encoder_draws(key)
    return states.astype(jnp.bfloat16)


def draw_norm_gain(key, part):
    states, gains, weight = encoder_draws(key)
    return gains


def draw_kv_weight(key, part):
    states, gains, weight = encoder_draws(key)
    return weight.astype(jnp.bfloat16)


def draw_queries(key, part):
    drawn = jnp.clip(jax.random.normal(jax.random.fold_in(key, 505), (DEC, H * HD), jnp.float32), -6.0, 6.0) * 2.5
    return drawn.astype(jnp.bfloat16)


def block_scale(rng, shape, split, smallest, top_value):
    loudness, own = 1.0, jax.random.fold_in(rng, 6)
    for position, parts in split:
        steps = jnp.exp(jax.random.uniform(jax.random.fold_in(own, position), (parts,), jnp.float32, smallest / len(split), top_value / len(split)))
        loudness = loudness * jnp.repeat(steps, shape[position] // parts).reshape([-1 if axis == position else 1 for axis in range(len(shape))])
    return loudness


def bell_draw(own_key, extent, spread, reach, split=(), kind=jnp.bfloat16):
    values = spread * jax.random.normal(own_key, extent, jnp.float32)
    if split:
        values = values * block_scale(own_key, extent, split, -0.22, 0.18)
    return jnp.clip(values, -reach, reach).astype(kind)


def setup_inputs(seed: int = 0) -> dict:
    streams_of = jax.random.split(jax.random.key(seed), 6)
    enc_states = draw_enc_states(jax.random.fold_in(streams_of[5], 71), 0)
    norm_gain = draw_norm_gain(jax.random.fold_in(streams_of[5], 71), 0)
    kv_weight = draw_kv_weight(jax.random.fold_in(streams_of[5], 71), 0)
    queries = draw_queries(jax.random.fold_in(streams_of[5], 71), 0)
    cotangent = bell_draw(streams_of[4], (DEC, H * HD), 2.0, 8.0, ((0, 8), (1, 4)))
    return dict(enc_states=enc_states, norm_gain=norm_gain, kv_weight=kv_weight, queries=queries, cotangent=cotangent)


def rounded(tensor):
    return lax.optimization_barrier(tensor.astype(jnp.bfloat16)).astype(jnp.float32)

def reference(enc_states, norm_gain, kv_weight, queries, cotangent):
    states = enc_states.astype(jnp.float32)
    inverse_root = lax.rsqrt(lax.optimization_barrier(jnp.mean(states * states, axis=1, keepdims=True)) + 1e-06)
    normed = (states * inverse_root * norm_gain).astype(jnp.bfloat16)
    keys_values = jnp.dot(normed, kv_weight, preferred_element_type=jnp.float32).astype(jnp.bfloat16)
    per_group = H // G
    factor = HD ** (-0.5)
    pieces = keys_values.astype(jnp.float32).reshape(ENC, G, 2, HD).transpose(1, 2, 0, 3)
    query_rows = queries.astype(jnp.float32).reshape(DEC, G, per_group, HD).transpose(1, 0, 2, 3).reshape(G, DEC * per_group, HD)
    grad_rows = cotangent.astype(jnp.float32).reshape(DEC, G, per_group, HD).transpose(1, 0, 2, 3).reshape(G, DEC * per_group, HD)
    row_count = DEC * per_group
    block_size = 1024 if row_count % 1024 == 0 else row_count
    highest = lax.Precision.HIGHEST

    def one_group(entries):
        query_group, grad_group, pair_group = entries
        key_rows = pair_group[0]
        values = pair_group[1]

        def advance(running, blocks):
            key_grad, value_grad = running
            query_block, grad_block = blocks
            scores = jnp.dot(query_block, key_rows.T, precision=highest) * factor
            row_max = lax.optimization_barrier(jnp.max(scores, axis=1, keepdims=True))
            exponent = jnp.exp(scores - row_max)
            totals = lax.optimization_barrier(jnp.sum(exponent, axis=1, keepdims=True))
            context = rounded(jnp.dot(rounded(exponent), values, precision=highest) / totals)
            probability = exponent / totals
            deltas = lax.optimization_barrier(jnp.sum(grad_block * context, axis=1, keepdims=True))
            prob_grad = jnp.dot(grad_block, values.T, precision=highest)
            score_grad = rounded(factor * probability * (prob_grad - deltas))
            query_grad = jnp.dot(score_grad, key_rows, precision=highest)
            key_grad = key_grad + jnp.dot(score_grad.T, query_block, precision=highest)
            value_grad = value_grad + jnp.dot(rounded(probability).T, grad_block, precision=highest)
            return ((key_grad, value_grad), (context, query_grad))
        empty_grad = jnp.zeros((ENC, HD), jnp.float32)
        blocks = (query_group.reshape(row_count // block_size, block_size, HD), grad_group.reshape(row_count // block_size, block_size, HD))
        (key_grad, value_grad), (context, query_grad) = lax.scan(advance, (empty_grad, empty_grad), blocks)
        return (context.reshape(row_count, HD), query_grad.reshape(row_count, HD), jnp.stack([key_grad, value_grad]))
    context, query_grad, pair_grad = lax.map(one_group, (query_rows, grad_rows, pieces))
    context = context.reshape(G, DEC, per_group, HD).transpose(1, 0, 2, 3).reshape(DEC, H * HD)
    query_grad = query_grad.reshape(G, DEC, per_group, HD).transpose(1, 0, 2, 3).reshape(DEC, H * HD)
    pair_grad = pair_grad.transpose(2, 0, 1, 3).reshape(ENC, 2 * G * HD)
    return (context.astype(jnp.bfloat16), query_grad.astype(jnp.bfloat16), pair_grad.astype(jnp.bfloat16))
```

```python
import functools
import math

import jax
import jax.numpy as jnp
from jax import lax
from jax.experimental import pallas as pl
from jax.experimental.pallas import tpu as pltpu
from jax.sharding import PartitionSpec as P

HD = 64
EPS = 1e-06
LOG2E = math.log2(math.e)
SCALE = HD ** (-0.5)
KEY_ROWS = 256
VMEM_BYTES = 60 << 20
NT = (((1,), (1,)), ((), ()))

bf16 = jnp.bfloat16
f32 = jnp.float32

IN_VMEM = pl.BlockSpec(memory_space=pltpu.VMEM)
IN_PLACE = pl.BlockSpec(memory_space=pl.ANY)


def project_kernel(x_ref, gain_ref, w_ref, out_ref):
    x = x_ref[...].astype(f32)
    inverse_root = lax.rsqrt(jnp.mean(x * x, axis=1, keepdims=True) + EPS)
    normed = (x * inverse_root * gain_ref[...]).astype(bf16)
    pairs = jnp.dot(normed, w_ref[...], preferred_element_type=f32).astype(bf16)
    for g in range(out_ref.shape[0]):
        out_ref[g] = pairs[:, g * 2 * HD : (g + 1) * 2 * HD]


def project(states, gain, weight):
    rows, width = states.shape
    groups = weight.shape[1] // (2 * HD)
    block = min(rows, 256)
    return pl.pallas_call(
        project_kernel,
        grid=(rows // block,),
        in_specs=[
            pl.BlockSpec((block, width), lambda i: (i, 0)),
            pl.BlockSpec((1, width), lambda i: (0, 0)),
            pl.BlockSpec((width, weight.shape[1]), lambda i: (0, 0)),
        ],
        out_specs=pl.BlockSpec((groups, block, 2 * HD), lambda i: (0, i, 0)),
        out_shape=jax.ShapeDtypeStruct((groups, rows, 2 * HD), bf16),
        compiler_params=pltpu.CompilerParams(vmem_limit_bytes=VMEM_BYTES),
        cost_estimate=pl.CostEstimate(
            flops=2 * rows * width * weight.shape[1], bytes_accessed=2 * rows * width, transcendentals=0
        ),
        name="project",
    )(states, gain.reshape(1, width), weight)


def turn_kernel(count, *refs):
    inputs, out_ref = refs[:count], refs[count]
    chunks, _, lanes = out_ref.shape
    per_block = chunks // count
    tokens = inputs[0].shape[0]
    heads = lanes // tokens
    for s in range(count):
        turned = inputs[s][...].T
        for i in range(per_block):
            base = i * heads * HD
            out_ref[s * per_block + i] = jnp.concatenate(
                [turned[base + h * HD : base + (h + 1) * HD] for h in range(heads)], axis=1
            )


def turn(blocks, heads):
    tokens, width = blocks[0].shape
    chunks = len(blocks) * width // (heads * HD)
    return pl.pallas_call(
        functools.partial(turn_kernel, len(blocks)),
        in_specs=[IN_VMEM] * len(blocks),
        out_specs=IN_VMEM,
        out_shape=jax.ShapeDtypeStruct((chunks, HD, heads * tokens), bf16),
        compiler_params=pltpu.CompilerParams(vmem_limit_bytes=VMEM_BYTES),
        name="turn",
    )(*blocks)


def forward_kernel(dims, first, last, *refs):
    chunks, groups, per_group = dims
    refs = list(refs)
    q_ref = refs.pop(0)
    c_ref = refs.pop(0) if last else None
    kv_ref = refs.pop(0)
    past, past_acc = (None, None) if first else (refs.pop(0), refs.pop(0))
    e_hbm, top_ref, st_ref, acc_ref, value_t, scores, expo, sem = refs
    length = kv_ref.shape[1]
    lanes = q_ref.shape[2]
    pad = jnp.zeros((HD, lanes), bf16)
    steps = length // KEY_ROWS
    for g in range(groups):
        value_t[g, :HD] = kv_ref[g].T[HD:]
        value_t[g, HD:] = jnp.ones((16, length), bf16)

    def group_of(c):
        return (c // per_group) % groups

    def store(slot, c):
        return pltpu.make_async_copy(expo.at[slot], e_hbm.at[c], sem.at[slot])

    def emit(ca, cb, cc, slot, top, wait):
        largest, total = None, None
        if ca is not None:
            weights = jnp.concatenate([q_ref[ca] * jnp.asarray(SCALE, bf16), pad], axis=0)
            ga = group_of(ca)
        if cb is not None:
            low_top = top * LOG2E
            if wait:
                store(slot, cb).wait()
        if cc is not None:
            gc = group_of(cc)
        for k in range(steps):
            ks = slice(k * KEY_ROWS, (k + 1) * KEY_ROWS)
            if cb is not None:
                expo[slot, ks] = jnp.exp2(scores[ks] * LOG2E - low_top).astype(bf16)
            if ca is not None:
                s = jnp.dot(kv_ref[ga, ks], weights, preferred_element_type=f32)
                scores[ks] = s
                part = jnp.max(s.reshape(KEY_ROWS // 8, 8, lanes), axis=0)
                largest = part if largest is None else jnp.maximum(largest, part)
            if cc is not None:
                part = jnp.dot(value_t[gc, :, ks], expo[1 - slot, ks], preferred_element_type=f32)
                total = part if total is None else total + part
        if cb is not None:
            top_ref[pl.ds(cb, 1)] = top
            store(slot, cb).start()
        if cc is not None:
            m = top_ref[pl.ds(cc, 1)]
            l = total[HD : HD + 1]
            acc = total[:HD]
            if not first:
                before = past[0, pl.ds(cc, 1)]
                both = jnp.maximum(before, m)
                old, new = jnp.exp(before - both), jnp.exp(m - both)
                l = past[1, pl.ds(cc, 1)] * old + l * new
                acc = past_acc[cc] * old + acc * new
                m = both
            st_ref[0, pl.ds(cc, 1)] = m
            st_ref[1, pl.ds(cc, 1)] = l
            if last:
                st_ref[2, pl.ds(cc, 1)] = jnp.sum(c_ref[cc].astype(f32) * acc, axis=0, keepdims=True)
            acc_ref[cc] = acc
        return None if largest is None else jnp.max(largest, axis=0, keepdims=True)

    n = chunks
    top = emit(0, None, None, None, None, False)
    top = emit(1, 0, None, 0, top, False)

    def body(j, top, wait=True):
        top = emit(2 * j + 2, 2 * j + 1, 2 * j, 1, top, wait)
        return emit(2 * j + 3, 2 * j + 2, 2 * j + 1, 0, top, True)

    top = body(0, top, wait=False)
    top = lax.fori_loop(1, n // 2 - 1, body, top)
    emit(None, n - 1, n - 2, 1, top, True)
    emit(None, None, n - 1, 0, None, False)
    store(0, n - 2).wait()
    store(1, n - 1).wait()


def forward(dims, q_rows, c_rows, pairs, before):
    chunks, groups, per_group = dims
    lanes = q_rows.shape[2]
    length = pairs.shape[1]
    first, last = before is None, c_rows is not None
    args = [q_rows] + ([c_rows] if last else []) + [pairs] + ([] if first else list(before))
    size = chunks * lanes * length
    return pl.pallas_call(
        functools.partial(forward_kernel, dims, first, last),
        in_specs=[IN_VMEM] * len(args),
        out_specs=[IN_PLACE, IN_VMEM, IN_VMEM, IN_VMEM],
        out_shape=[
            jax.ShapeDtypeStruct((chunks, length, lanes), bf16),
            jax.ShapeDtypeStruct((chunks, lanes), f32),
            jax.ShapeDtypeStruct((3 if last else 2, chunks, lanes), f32),
            jax.ShapeDtypeStruct((chunks, HD, lanes), f32),
        ],
        scratch_shapes=[
            pltpu.VMEM((groups, HD + 16, length), bf16),
            pltpu.VMEM((length, lanes), f32),
            pltpu.VMEM((2, length, lanes), bf16),
            pltpu.SemaphoreType.DMA((2,)),
        ],
        compiler_params=pltpu.CompilerParams(vmem_limit_bytes=VMEM_BYTES),
        cost_estimate=pl.CostEstimate(flops=16 * size * HD, bytes_accessed=2 * size, transcendentals=size),
        name="forward",
    )(*args)


def rolled(rows, shift):
    count = rows.shape[0]
    shift = shift % count
    return rows if shift == 0 else jnp.concatenate([rows[count - shift :], rows[: count - shift]], axis=0)


def backward_kernel(dims, peers, first, last, *refs):
    chunks, groups, per_group = dims
    refs = list(refs)
    q_ref, c_ref, kv_ref, e_hbm, top_ref, own_ref = [refs.pop(0) for _ in range(6)]
    peer_refs = [refs.pop(0) for _ in range(peers)]
    acc_ref = refs.pop(0) if first else None
    past_dq = None if first else refs.pop(0)
    blocks = peers + 1
    ctx_outs = [refs.pop(0) for _ in range(blocks)] if first else None
    dq_outs = [refs.pop(0) for _ in range(blocks)] if last else [refs.pop(0)]
    dkv_ref = refs.pop(0)
    key_t, expo, score_grad, key_sum, value_sum, factor, delta, rows, sem, row_sem = refs
    length = kv_ref.shape[1]
    lanes = q_ref.shape[2]
    steps = length // KEY_ROWS
    heads = per_block_heads = lanes // rows.shape[1]
    per_block = chunks // blocks
    pad = jnp.zeros((HD, lanes), bf16)

    def group_of(c):
        return (c // per_group) % groups

    def fetch(slot, c):
        return pltpu.make_async_copy(e_hbm.at[c], expo.at[slot], sem.at[slot])

    fetch(0, 0).start()
    fetch(1, 1).start()
    for g in range(groups):
        key_t[g] = kv_ref[g].T[:HD]
    key_sum[...] = jnp.zeros_like(key_sum)
    value_sum[...] = jnp.zeros_like(value_sum)

    stats = [[own_ref[i] for i in range(3)]]
    for r in range(1, blocks):
        stats.append([rolled(peer_refs[r - 1][i], r * per_block) for i in range(3)])
    top = functools.reduce(jnp.maximum, [s[0] for s in stats])
    shares = [jnp.exp(s[0] - top) for s in stats]
    total = sum(s[1] * w for s, w in zip(stats, shares))
    delta[...] = sum(s[2] * w for s, w in zip(stats, shares)) / total
    factor[0] = jnp.exp(top_ref[...] - top) / total
    if first:
        factor[1] = shares[0] / total

    def put_rows(c, value):
        flat = jnp.concatenate([value[:, h * rows.shape[1] : (h + 1) * rows.shape[1]] for h in range(heads)], axis=0)
        offset = pl.multiple_of((c % per_block) * heads * HD, heads * HD)
        rows[c // per_block, :, pl.ds(offset, heads * HD)] = flat.astype(bf16).T

    def send_rows(outs):
        copies = [pltpu.make_async_copy(rows.at[s], outs[s], row_sem.at[s]) for s in range(blocks)]
        for copy in copies:
            copy.start()
        for copy in copies:
            copy.wait()

    if first:

        def put_context(c, _):
            put_rows(c, acc_ref[c] * factor[1, pl.ds(c, 1)])
            return 0

        lax.fori_loop(0, chunks, put_context, 0)
        send_rows(ctx_outs)

    def emit(ca, cb, slot):
        if ca is not None:
            ga = group_of(ca)
            weights = jnp.concatenate([pad, c_ref[ca]], axis=0)
            fa, da = factor[0, pl.ds(ca, 1)], delta[pl.ds(ca, 1)]
            scaled_c = (c_ref[ca].astype(f32) * fa).astype(bf16)
            fetch(slot, ca).wait()
        if cb is not None:
            gb = group_of(cb)
            fb = factor[0, pl.ds(cb, 1)] * SCALE
            scaled_q = (q_ref[cb].astype(f32) * fb).astype(bf16)
            dq = None
        for k in range(steps):
            ks = slice(k * KEY_ROWS, (k + 1) * KEY_ROWS)
            if cb is not None:
                ds = score_grad[ks]
                part = jnp.dot(key_t[gb, :, ks], ds, preferred_element_type=f32)
                dq = part if dq is None else dq + part
                key_sum[gb, :, ks] += lax.dot_general(scaled_q, ds, NT, preferred_element_type=f32)
            if ca is not None:
                e = expo[slot, ks]
                prob_grad = jnp.dot(kv_ref[ga, ks], weights, preferred_element_type=f32)
                score_grad[ks] = (e.astype(f32) * (prob_grad - da)).astype(bf16)
                value_sum[ga, :, ks] += lax.dot_general(scaled_c, e, NT, preferred_element_type=f32)
        if cb is not None:
            dq = dq * fb
            if not first:
                dq = dq + past_dq[cb]
            if last:
                put_rows(cb, dq)
            else:
                dq_outs[0][cb] = dq

    n = chunks
    emit(0, None, 0)

    def body(j, _):
        @pl.when(2 * j + 2 < n)
        def _():
            fetch(0, 2 * j + 2).start()

        emit(2 * j + 1, 2 * j, 1)

        @pl.when(2 * j + 2 < n)
        def _():
            fetch(1, 2 * j + 3).start()
            emit(2 * j + 2, 2 * j + 1, 0)

        return 0

    lax.fori_loop(0, n // 2, body, 0)
    emit(None, n - 1, None)
    if last:
        send_rows(dq_outs)
    for g in range(groups):
        both = jnp.concatenate([key_sum[g], value_sum[g]], axis=0)
        dkv_ref[:, g * 2 * HD : (g + 1) * 2 * HD] = both.T.astype(dkv_ref.dtype)


def backward(dims, q_rows, c_rows, pairs, expo, top, own, peers, acc, past_dq, last, tokens):
    chunks, groups, per_group = dims
    lanes = q_rows.shape[2]
    length = pairs.shape[1]
    first = past_dq is None
    blocks = len(peers) + 1
    width = chunks // blocks * (lanes // tokens) * HD
    args = [q_rows, c_rows, pairs, expo, top, own, *peers] + [acc if first else past_dq]
    specs = [IN_VMEM] * 3 + [IN_PLACE] + [IN_VMEM] * (len(args) - 4)
    row_block = jax.ShapeDtypeStruct((tokens, width), bf16)
    outs, out_specs = [], []
    if first:
        outs += [row_block] * blocks
        out_specs += [IN_PLACE] * blocks
    if last:
        outs += [row_block] * blocks
        out_specs += [IN_PLACE] * blocks
    else:
        outs.append(jax.ShapeDtypeStruct((chunks, HD, lanes), f32))
        out_specs.append(IN_VMEM)
    outs.append(jax.ShapeDtypeStruct((length, groups * 2 * HD), f32 if last else bf16))
    out_specs.append(IN_VMEM)
    size = chunks * lanes * length
    results = list(
        pl.pallas_call(
            functools.partial(backward_kernel, dims, len(peers), first, last),
            in_specs=specs,
            out_specs=out_specs,
            out_shape=outs,
            scratch_shapes=[
                pltpu.VMEM((groups, HD, length), bf16),
                pltpu.VMEM((2, length, lanes), bf16),
                pltpu.VMEM((length, lanes), bf16),
                pltpu.VMEM((groups, HD, length), f32),
                pltpu.VMEM((groups, HD, length), f32),
                pltpu.VMEM((2, chunks, lanes), f32),
                pltpu.VMEM((chunks, lanes), f32),
                pltpu.VMEM((blocks, tokens, width), bf16),
                pltpu.SemaphoreType.DMA((2,)),
                pltpu.SemaphoreType.DMA((blocks,)),
            ],
            compiler_params=pltpu.CompilerParams(vmem_limit_bytes=VMEM_BYTES),
            cost_estimate=pl.CostEstimate(flops=24 * size * HD, bytes_accessed=2 * size, transcendentals=0),
            name="backward",
        )(*args)
    )
    context = [results.pop(0) for _ in range(blocks)] if first else None
    dq = [results.pop(0) for _ in range(blocks)] if last else results.pop(0)
    return context, dq, results.pop(0)


def on_device(halves, seqs, enc_states, norm_gain, kv_weight, queries, cotangent):
    tokens, width = queries.shape
    groups = kv_weight.shape[1] // (2 * HD)
    per_group_heads = width // (groups * HD)
    heads = min(per_group_heads, max(1, 512 // tokens))
    per_group = per_group_heads // heads
    chunks = seqs * groups * per_group
    dims = (chunks, groups, per_group)

    def from_seq(x, shift):
        return lax.ppermute(x, "seq", [(i, (i + shift) % seqs) for i in range(seqs)])

    def from_half(x, shift):
        return lax.ppermute(x, "half", [(i, (i + shift) % halves) for i in range(halves)])

    q_blocks = [queries] + [from_seq(queries, s) for s in range(1, seqs)]
    late, *_ = lax.optimization_barrier((cotangent, *q_blocks[1:]))
    c_blocks = [late] + [from_seq(late, s) for s in range(1, seqs)]
    own_pairs = project(enc_states, norm_gain, kv_weight)
    pair_blocks = [own_pairs] + [from_half(own_pairs, s) for s in range(1, halves)]
    q_rows = turn(q_blocks, heads)
    c_rows = turn(c_blocks, heads)

    expos, tops, before = [], [], None
    for i, pairs in enumerate(pair_blocks):
        expo, top, stats, acc = forward(dims, q_rows, c_rows if i == halves - 1 else None, pairs, before)
        expos.append(expo)
        tops.append(top)
        before = (stats, acc)
    peers = [from_seq(stats, r) for r in range(1, seqs)]

    dq, sends, context_parts = None, [], None
    for i in reversed(range(halves)):
        parts, dq, dkv = backward(
            dims, q_rows, c_rows, pair_blocks[i], expos[i], tops[i], stats, peers, acc, dq, i == 0, tokens
        )
        if parts is not None:
            context_parts = parts
        sends.append(dkv if i == 0 else from_half(dkv, -i))

    def home(parts):
        arrived = [parts[0]] + [from_seq(parts[s], -s) for s in range(1, seqs)]
        return sum(x.astype(f32) for x in arrived).astype(bf16)

    context = home(context_parts)
    d_queries = home(dq)
    d_pairs = sum(x.astype(f32) for x in sends).astype(bf16)
    return (context, d_queries, d_pairs)


def solution(mesh):
    shape = mesh.shape
    rows, columns = P(("half", "seq"), None), P(("half", "seq"), "head")
    return jax.shard_map(
        functools.partial(on_device, shape["half"], shape["seq"]),
        mesh=mesh,
        in_specs=(rows, P(), P(None, "head"), columns, columns),
        out_specs=(columns, columns, columns),
        check_vma=False,
    )
```

```python
import functools
import math

import jax
import jax.numpy as jnp
from jax import lax
from jax.experimental import pallas as pl
from jax.experimental.pallas import tpu as pltpu
from jax.sharding import PartitionSpec as P

HD = 64
EPS = 1e-06
LOG2E = math.log2(math.e)
SCALE = HD ** (-0.5)
KEY_ROWS = 256
VMEM_BYTES = 60 << 20
NT = (((1,), (1,)), ((), ()))

bf16 = jnp.bfloat16
f32 = jnp.float32

IN_VMEM = pl.BlockSpec(memory_space=pltpu.VMEM)
IN_PLACE = pl.BlockSpec(memory_space=pl.ANY)


def project_kernel(x_ref, gain_ref, w_ref, out_ref):
    x = x_ref[...].astype(f32)
    inverse_root = lax.rsqrt(jnp.mean(x * x, axis=1, keepdims=True) + EPS)
    normed = (x * inverse_root * gain_ref[...]).astype(bf16)
    pairs = jnp.dot(normed, w_ref[...], preferred_element_type=f32).astype(bf16)
    for g in range(out_ref.shape[0]):
        out_ref[g] = pairs[:, g * 2 * HD : (g + 1) * 2 * HD]


def project(states, gain, weight):
    rows, width = states.shape
    groups = weight.shape[1] // (2 * HD)
    block = min(rows, 256)
    return pl.pallas_call(
        project_kernel,
        grid=(rows // block,),
        in_specs=[
            pl.BlockSpec((block, width), lambda i: (i, 0)),
            pl.BlockSpec((1, width), lambda i: (0, 0)),
            pl.BlockSpec((width, weight.shape[1]), lambda i: (0, 0)),
        ],
        out_specs=pl.BlockSpec((groups, block, 2 * HD), lambda i: (0, i, 0)),
        out_shape=jax.ShapeDtypeStruct((groups, rows, 2 * HD), bf16),
        compiler_params=pltpu.CompilerParams(vmem_limit_bytes=VMEM_BYTES),
        cost_estimate=pl.CostEstimate(
            flops=2 * rows * width * weight.shape[1], bytes_accessed=2 * rows * width, transcendentals=0
        ),
        name="project",
    )(states, gain.reshape(1, width), weight)


def turn_kernel(count, *refs):
    inputs, out_ref = refs[:count], refs[count]
    chunks, _, lanes = out_ref.shape
    per_block = chunks // count
    tokens = inputs[0].shape[0]
    heads = lanes // tokens
    for s in range(count):
        turned = inputs[s][...].T
        for i in range(per_block):
            base = i * heads * HD
            out_ref[s * per_block + i] = jnp.concatenate(
                [turned[base + h * HD : base + (h + 1) * HD] for h in range(heads)], axis=1
            )


def turn(blocks, heads):
    tokens, width = blocks[0].shape
    chunks = len(blocks) * width // (heads * HD)
    return pl.pallas_call(
        functools.partial(turn_kernel, len(blocks)),
        in_specs=[IN_VMEM] * len(blocks),
        out_specs=IN_VMEM,
        out_shape=jax.ShapeDtypeStruct((chunks, HD, heads * tokens), bf16),
        compiler_params=pltpu.CompilerParams(vmem_limit_bytes=VMEM_BYTES),
        name="turn",
    )(*blocks)


def forward_kernel(dims, first, last, *refs):
    chunks, groups, per_group = dims
    refs = list(refs)
    q_ref = refs.pop(0)
    c_ref = refs.pop(0) if last else None
    kv_ref = refs.pop(0)
    past, past_acc = (None, None) if first else (refs.pop(0), refs.pop(0))
    e_hbm, top_ref, st_ref, acc_ref, value_t, scores, expo, sem = refs
    length = kv_ref.shape[1]
    lanes = q_ref.shape[2]
    pad = jnp.zeros((HD, lanes), bf16)
    steps = length // KEY_ROWS
    for g in range(groups):
        value_t[g, :HD] = kv_ref[g].T[HD:]
        value_t[g, HD:] = jnp.ones((16, length), bf16)

    def group_of(c):
        return (c // per_group) % groups

    def store(slot, c):
        return pltpu.make_async_copy(expo.at[slot], e_hbm.at[c], sem.at[slot])

    def emit(ca, cb, cc, slot, top, wait):
        largest, total = None, None
        if ca is not None:
            weights = jnp.concatenate([q_ref[ca] * jnp.asarray(SCALE, bf16), pad], axis=0)
            ga = group_of(ca)
        if cb is not None:
            low_top = top * LOG2E
            if wait:
                store(slot, cb).wait()
        if cc is not None:
            gc = group_of(cc)
        for k in range(steps):
            ks = slice(k * KEY_ROWS, (k + 1) * KEY_ROWS)
            if cb is not None:
                expo[slot, ks] = jnp.exp2(scores[ks] * LOG2E - low_top).astype(bf16)
            if ca is not None:
                s = jnp.dot(kv_ref[ga, ks], weights, preferred_element_type=f32)
                scores[ks] = s
                part = jnp.max(s.reshape(KEY_ROWS // 8, 8, lanes), axis=0)
                largest = part if largest is None else jnp.maximum(largest, part)
            if cc is not None:
                part = jnp.dot(value_t[gc, :, ks], expo[1 - slot, ks], preferred_element_type=f32)
                total = part if total is None else total + part
        if cb is not None:
            top_ref[pl.ds(cb, 1)] = top
            store(slot, cb).start()
        if cc is not None:
            m = top_ref[pl.ds(cc, 1)]
            l = total[HD : HD + 1]
            acc = total[:HD]
            if not first:
                before = past[0, pl.ds(cc, 1)]
                both = jnp.maximum(before, m)
                old, new = jnp.exp(before - both), jnp.exp(m - both)
                l = past[1, pl.ds(cc, 1)] * old + l * new
                acc = past_acc[cc] * old + acc * new
                m = both
            st_ref[0, pl.ds(cc, 1)] = m
            st_ref[1, pl.ds(cc, 1)] = l
            if last:
                st_ref[2, pl.ds(cc, 1)] = jnp.sum(c_ref[cc].astype(f32) * acc, axis=0, keepdims=True)
            acc_ref[cc] = acc
        return None if largest is None else jnp.max(largest, axis=0, keepdims=True)

    n = chunks
    top = emit(0, None, None, None, None, False)
    top = emit(1, 0, None, 0, top, False)

    def body(j, top, wait=True):
        top = emit(2 * j + 2, 2 * j + 1, 2 * j, 1, top, wait)
        return emit(2 * j + 3, 2 * j + 2, 2 * j + 1, 0, top, True)

    top = body(0, top, wait=False)
    top = lax.fori_loop(1, n // 2 - 1, body, top)
    emit(None, n - 1, n - 2, 1, top, True)
    emit(None, None, n - 1, 0, None, False)
    store(0, n - 2).wait()
    store(1, n - 1).wait()


def forward(dims, q_rows, c_rows, pairs, before):
    chunks, groups, per_group = dims
    lanes = q_rows.shape[2]
    length = pairs.shape[1]
    first, last = before is None, c_rows is not None
    args = [q_rows] + ([c_rows] if last else []) + [pairs] + ([] if first else list(before))
    size = chunks * lanes * length
    return pl.pallas_call(
        functools.partial(forward_kernel, dims, first, last),
        in_specs=[IN_VMEM] * len(args),
        out_specs=[IN_PLACE, IN_VMEM, IN_VMEM, IN_VMEM],
        out_shape=[
            jax.ShapeDtypeStruct((chunks, length, lanes), bf16),
            jax.ShapeDtypeStruct((chunks, lanes), f32),
            jax.ShapeDtypeStruct((3 if last else 2, chunks, lanes), f32),
            jax.ShapeDtypeStruct((chunks, HD, lanes), f32),
        ],
        scratch_shapes=[
            pltpu.VMEM((groups, HD + 16, length), bf16),
            pltpu.VMEM((length, lanes), f32),
            pltpu.VMEM((2, length, lanes), bf16),
            pltpu.SemaphoreType.DMA((2,)),
        ],
        compiler_params=pltpu.CompilerParams(vmem_limit_bytes=VMEM_BYTES),
        cost_estimate=pl.CostEstimate(flops=16 * size * HD, bytes_accessed=2 * size, transcendentals=size),
        name="forward",
    )(*args)


def rolled(rows, shift):
    count = rows.shape[0]
    shift = shift % count
    return rows if shift == 0 else jnp.concatenate([rows[count - shift :], rows[: count - shift]], axis=0)


def backward_kernel(dims, peers, first, last, *refs):
    chunks, groups, per_group = dims
    refs = list(refs)
    q_ref, c_ref, kv_ref, e_hbm, top_ref, own_ref = [refs.pop(0) for _ in range(6)]
    peer_refs = [refs.pop(0) for _ in range(peers)]
    acc_ref = refs.pop(0) if first else None
    past_dq = None if first else refs.pop(0)
    blocks = peers + 1
    ctx_outs = [refs.pop(0) for _ in range(blocks)] if first else None
    dq_outs = [refs.pop(0) for _ in range(blocks)] if last else [refs.pop(0)]
    dkv_ref = refs.pop(0)
    key_t, expo, score_grad, key_sum, value_sum, factor, delta, rows, sem, row_sem = refs
    length = kv_ref.shape[1]
    lanes = q_ref.shape[2]
    steps = length // KEY_ROWS
    heads = per_block_heads = lanes // rows.shape[1]
    per_block = chunks // blocks
    pad = jnp.zeros((HD, lanes), bf16)

    def group_of(c):
        return (c // per_group) % groups

    def fetch(slot, c):
        return pltpu.make_async_copy(e_hbm.at[c], expo.at[slot], sem.at[slot])

    fetch(0, 0).start()
    fetch(1, 1).start()
    for g in range(groups):
        key_t[g] = kv_ref[g].T[:HD]
    key_sum[...] = jnp.zeros_like(key_sum)
    value_sum[...] = jnp.zeros_like(value_sum)

    stats = [[own_ref[i] for i in range(3)]]
    for r in range(1, blocks):
        stats.append([rolled(peer_refs[r - 1][i], r * per_block) for i in range(3)])
    top = functools.reduce(jnp.maximum, [s[0] for s in stats])
    shares = [jnp.exp(s[0] - top) for s in stats]
    total = sum(s[1] * w for s, w in zip(stats, shares))
    delta[...] = sum(s[2] * w for s, w in zip(stats, shares)) / total
    factor[0] = jnp.exp(top_ref[...] - top) / total
    if first:
        factor[1] = shares[0] / total

    def put_rows(c, value):
        flat = jnp.concatenate([value[:, h * rows.shape[1] : (h + 1) * rows.shape[1]] for h in range(heads)], axis=0)
        offset = pl.multiple_of((c % per_block) * heads * HD, heads * HD)
        rows[c // per_block, :, pl.ds(offset, heads * HD)] = flat.astype(bf16).T

    def send_rows(outs):
        copies = [pltpu.make_async_copy(rows.at[s], outs[s], row_sem.at[s]) for s in range(blocks)]
        for copy in copies:
            copy.start()
        for copy in copies:
            copy.wait()

    if first:

        def put_context(c, _):
            put_rows(c, acc_ref[c] * factor[1, pl.ds(c, 1)])
            return 0

        lax.fori_loop(0, chunks, put_context, 0)
        send_rows(ctx_outs)

    def emit(ca, cb, slot):
        if ca is not None:
            ga = group_of(ca)
            weights = jnp.concatenate([pad, c_ref[ca]], axis=0)
            fa, da = factor[0, pl.ds(ca, 1)], delta[pl.ds(ca, 1)]
            scaled_c = (c_ref[ca].astype(f32) * fa).astype(bf16)
            fetch(slot, ca).wait()
        if cb is not None:
            gb = group_of(cb)
            fb = factor[0, pl.ds(cb, 1)] * SCALE
            scaled_q = (q_ref[cb].astype(f32) * fb).astype(bf16)
            dq = None
        for k in range(steps):
            ks = slice(k * KEY_ROWS, (k + 1) * KEY_ROWS)
            if cb is not None:
                ds = score_grad[ks]
                part = jnp.dot(key_t[gb, :, ks], ds, preferred_element_type=f32)
                dq = part if dq is None else dq + part
                key_sum[gb, :, ks] += lax.dot_general(scaled_q, ds, NT, preferred_element_type=f32)
            if ca is not None:
                e = expo[slot, ks]
                prob_grad = jnp.dot(kv_ref[ga, ks], weights, preferred_element_type=f32)
                score_grad[ks] = (e.astype(f32) * (prob_grad - da)).astype(bf16)
                value_sum[ga, :, ks] += lax.dot_general(scaled_c, e, NT, preferred_element_type=f32)
        if cb is not None:
            dq = dq * fb
            if not first:
                dq = dq + past_dq[cb]
            if last:
                put_rows(cb, dq)
            else:
                dq_outs[0][cb] = dq

    n = chunks
    emit(0, None, 0)

    def body(j, _):
        @pl.when(2 * j + 2 < n)
        def _():
            fetch(0, 2 * j + 2).start()

        emit(2 * j + 1, 2 * j, 1)

        @pl.when(2 * j + 2 < n)
        def _():
            fetch(1, 2 * j + 3).start()
            emit(2 * j + 2, 2 * j + 1, 0)

        return 0

    lax.fori_loop(0, n // 2, body, 0)
    emit(None, n - 1, None)
    if last:
        send_rows(dq_outs)
    for g in range(groups):
        both = jnp.concatenate([key_sum[g], value_sum[g]], axis=0)
        dkv_ref[:, g * 2 * HD : (g + 1) * 2 * HD] = both.T.astype(dkv_ref.dtype)


def backward(dims, q_rows, c_rows, pairs, expo, top, own, peers, acc, past_dq, last, tokens):
    chunks, groups, per_group = dims
    lanes = q_rows.shape[2]
    length = pairs.shape[1]
    first = past_dq is None
    blocks = len(peers) + 1
    width = chunks // blocks * (lanes // tokens) * HD
    args = [q_rows, c_rows, pairs, expo, top, own, *peers] + [acc if first else past_dq]
    specs = [IN_VMEM] * 3 + [IN_PLACE] + [IN_VMEM] * (len(args) - 4)
    row_block = jax.ShapeDtypeStruct((tokens, width), bf16)
    outs, out_specs = [], []
    if first:
        outs += [row_block] * blocks
        out_specs += [IN_PLACE] * blocks
    if last:
        outs += [row_block] * blocks
        out_specs += [IN_PLACE] * blocks
    else:
        outs.append(jax.ShapeDtypeStruct((chunks, HD, lanes), f32))
        out_specs.append(IN_VMEM)
    outs.append(jax.ShapeDtypeStruct((length, groups * 2 * HD), f32 if last else bf16))
    out_specs.append(IN_VMEM)
    size = chunks * lanes * length
    results = list(
        pl.pallas_call(
            functools.partial(backward_kernel, dims, len(peers), first, last),
            in_specs=specs,
            out_specs=out_specs,
            out_shape=outs,
            scratch_shapes=[
                pltpu.VMEM((groups, HD, length), bf16),
                pltpu.VMEM((2, length, lanes), bf16),
                pltpu.VMEM((length, lanes), bf16),
                pltpu.VMEM((groups, HD, length), f32),
                pltpu.VMEM((groups, HD, length), f32),
                pltpu.VMEM((2, chunks, lanes), f32),
                pltpu.VMEM((chunks, lanes), f32),
                pltpu.VMEM((blocks, tokens, width), bf16),
                pltpu.SemaphoreType.DMA((2,)),
                pltpu.SemaphoreType.DMA((blocks,)),
            ],
            compiler_params=pltpu.CompilerParams(vmem_limit_bytes=VMEM_BYTES),
            cost_estimate=pl.CostEstimate(flops=24 * size * HD, bytes_accessed=2 * size, transcendentals=0),
            name="backward",
        )(*args)
    )
    context = [results.pop(0) for _ in range(blocks)] if first else None
    dq = [results.pop(0) for _ in range(blocks)] if last else results.pop(0)
    return context, dq, results.pop(0)


def on_device(halves, seqs, enc_states, norm_gain, kv_weight, queries, cotangent):
    tokens, width = queries.shape
    groups = kv_weight.shape[1] // (2 * HD)
    per_group_heads = width // (groups * HD)
    heads = min(per_group_heads, max(1, 512 // tokens))
    per_group = per_group_heads // heads
    chunks = halves * groups * per_group
    dims = (chunks, groups, per_group)

    def from_seq(x, shift):
        return lax.ppermute(x, "seq", [(i, (i + shift) % seqs) for i in range(seqs)])

    def from_half(x, shift):
        return lax.ppermute(x, "half", [(i, (i + shift) % halves) for i in range(halves)])

    q_blocks = [queries] + [from_half(queries, s) for s in range(1, halves)]
    c_blocks = [cotangent] + [from_half(cotangent, s) for s in range(1, halves)]
    own_pairs = project(enc_states, norm_gain, kv_weight)
    order = sorted(range(seqs), key=lambda s: min(s, seqs - s))
    pair_blocks = [own_pairs] + [from_seq(own_pairs, s) for s in order[1:]]
    q_rows = turn(q_blocks, heads)
    c_rows = turn(c_blocks, heads)

    expos, tops, before = [], [], None
    for i, pairs in enumerate(pair_blocks):
        expo, top, stats, acc = forward(dims, q_rows, c_rows if i == seqs - 1 else None, pairs, before)
        expos.append(expo)
        tops.append(top)
        before = (stats, acc)
    peers = [from_half(stats, r) for r in range(1, halves)]

    dq, sends, context_parts = None, [], None
    for i in reversed(range(seqs)):
        parts, dq, dkv = backward(
            dims, q_rows, c_rows, pair_blocks[i], expos[i], tops[i], stats, peers, acc, dq, i == 0, tokens
        )
        if parts is not None:
            context_parts = parts
        sends.append(dkv if i == 0 else from_seq(dkv, -order[i]))

    def home(parts):
        arrived = [parts[0]] + [from_half(parts[s], -s) for s in range(1, halves)]
        return sum(x.astype(f32) for x in arrived).astype(bf16)

    context = home(context_parts)
    d_queries = home(dq)
    d_pairs = sum(x.astype(f32) for x in sends).astype(bf16)
    return (context, d_queries, d_pairs)


def solution(mesh):
    shape = mesh.shape
    rows, columns = P(("half", "seq"), None), P(("half", "seq"), "head")
    return jax.shard_map(
        functools.partial(on_device, shape["half"], shape["seq"]),
        mesh=mesh,
        in_specs=(rows, P(), P(None, "head"), columns, columns),
        out_specs=(columns, columns, columns),
        check_vma=False,
    )
```

```python
import functools
import math

import jax
import jax.numpy as jnp
from jax import lax
from jax.experimental import pallas as pl
from jax.experimental.pallas import tpu as pltpu
from jax.sharding import PartitionSpec as P


HD = 64
EPS = 1e-06
LOG2E = math.log2(math.e)
SCALE = HD ** (-0.5)
KEY_ROWS = 256
VMEM_BYTES = 14 << 20
NT = (((1,), (1,)), ((), ()))

bf16 = jnp.bfloat16
f32 = jnp.float32

IN_VMEM = pl.BlockSpec(memory_space=pltpu.VMEM)
IN_PLACE = pl.BlockSpec(memory_space=pl.ANY)


def project_kernel(x_ref, gain_ref, w_ref, out_ref):
    x = x_ref[...].astype(f32)
    inverse_root = lax.rsqrt(jnp.mean(x * x, axis=1, keepdims=True) + EPS)
    normed = (x * inverse_root * gain_ref[...]).astype(bf16)
    pairs = jnp.dot(normed, w_ref[...], preferred_element_type=f32).astype(bf16)
    for g in range(out_ref.shape[0]):
        out_ref[g] = pairs[:, g * 2 * HD : (g + 1) * 2 * HD]


def project(states, gain, weight):
    rows, width = states.shape
    groups = weight.shape[1] // (2 * HD)
    block = min(rows, 256)
    return pl.pallas_call(
        project_kernel,
        grid=(rows // block,),
        in_specs=[
            pl.BlockSpec((block, width), lambda i: (i, 0)),
            pl.BlockSpec((1, width), lambda i: (0, 0)),
            pl.BlockSpec((width, weight.shape[1]), lambda i: (0, 0)),
        ],
        out_specs=pl.BlockSpec((groups, block, 2 * HD), lambda i: (0, i, 0)),
        out_shape=jax.ShapeDtypeStruct((groups, rows, 2 * HD), bf16),
        compiler_params=pltpu.CompilerParams(vmem_limit_bytes=60 << 20),
        cost_estimate=pl.CostEstimate(
            flops=2 * rows * width * weight.shape[1], bytes_accessed=2 * rows * width, transcendentals=0
        ),
        name="project",
    )(states, gain.reshape(1, width), weight)


def turn_kernel(count, *refs):
    inputs, out_ref = refs[:count], refs[count]
    chunks, _, lanes = out_ref.shape
    per_block = chunks // count
    tokens = inputs[0].shape[0]
    heads = lanes // tokens
    for s in range(count):
        turned = inputs[s][...].T
        for i in range(per_block):
            base = i * heads * HD
            out_ref[s * per_block + i] = jnp.concatenate(
                [turned[base + h * HD : base + (h + 1) * HD] for h in range(heads)], axis=1
            )


def turn(blocks, heads):
    tokens, width = blocks[0].shape
    chunks = len(blocks) * width // (heads * HD)
    return pl.pallas_call(
        functools.partial(turn_kernel, len(blocks)),
        in_specs=[IN_VMEM] * len(blocks),
        out_specs=IN_VMEM,
        out_shape=jax.ShapeDtypeStruct((chunks, HD, heads * tokens), bf16),
        compiler_params=pltpu.CompilerParams(vmem_limit_bytes=VMEM_BYTES),
        name="turn",
    )(*blocks)


def gathered(piece_refs, whole_ref):
    if len(piece_refs) == 1:
        return piece_refs[0]
    begin = 0
    for piece in piece_refs:
        rows = piece.shape[1]
        whole_ref[:, begin : begin + rows] = piece[...]
        begin += rows
    return whole_ref


def forward_kernel(dims, pieces, first, last, *refs):
    chunks, groups, per_group = dims
    refs = list(refs)
    q_ref = refs.pop(0)
    c_ref = refs.pop(0) if last else None
    piece_refs = [refs.pop(0) for _ in range(pieces)]
    past, past_acc = (None, None) if first else (refs.pop(0), refs.pop(0))
    e_hbm, top_ref, st_ref, acc_ref, whole_ref, value_t, scores, expo, sem = refs
    kv_ref = gathered(piece_refs, whole_ref)
    length = kv_ref.shape[1]
    lanes = q_ref.shape[2]
    pad = jnp.zeros((HD, lanes), bf16)
    steps = length // KEY_ROWS
    for g in range(groups):
        value_t[g, :HD] = kv_ref[g].T[HD:]
        value_t[g, HD:] = jnp.ones((16, length), bf16)

    def group_of(c):
        return (c // per_group) % groups

    def store(slot, c):
        return pltpu.make_async_copy(expo.at[slot], e_hbm.at[c], sem.at[slot])

    def emit(ca, cb, cc, slot, top, wait):
        largest, total = None, None
        if ca is not None:
            weights = jnp.concatenate([q_ref[ca] * jnp.asarray(SCALE, bf16), pad], axis=0)
            ga = group_of(ca)
        if cb is not None:
            low_top = top * LOG2E
            if wait:
                store(slot, cb).wait()
        if cc is not None:
            gc = group_of(cc)
        for k in range(steps):
            ks = slice(k * KEY_ROWS, (k + 1) * KEY_ROWS)
            if cb is not None:
                expo[slot, ks] = jnp.exp2(scores[ks] * LOG2E - low_top).astype(bf16)
            if ca is not None:
                s = jnp.dot(kv_ref[ga, ks], weights, preferred_element_type=f32)
                scores[ks] = s
                part = jnp.max(s.reshape(KEY_ROWS // 8, 8, lanes), axis=0)
                largest = part if largest is None else jnp.maximum(largest, part)
            if cc is not None:
                part = jnp.dot(value_t[gc, :, ks], expo[1 - slot, ks], preferred_element_type=f32)
                total = part if total is None else total + part
        if cb is not None:
            top_ref[pl.ds(cb, 1)] = top
            store(slot, cb).start()
        if cc is not None:
            m = top_ref[pl.ds(cc, 1)]
            l = total[HD : HD + 1]
            acc = total[:HD]
            if not first:
                before = past[0, pl.ds(cc, 1)]
                both = jnp.maximum(before, m)
                old, new = jnp.exp(before - both), jnp.exp(m - both)
                l = past[1, pl.ds(cc, 1)] * old + l * new
                acc = past_acc[cc] * old + acc * new
                m = both
            st_ref[0, pl.ds(cc, 1)] = m
            st_ref[1, pl.ds(cc, 1)] = l
            if last:
                st_ref[2, pl.ds(cc, 1)] = jnp.sum(c_ref[cc].astype(f32) * acc, axis=0, keepdims=True)
            acc_ref[cc] = acc
        return None if largest is None else jnp.max(largest, axis=0, keepdims=True)

    n = chunks
    top = emit(0, None, None, None, None, False)
    top = emit(1, 0, None, 0, top, False)

    def body(j, top, wait=True):
        top = emit(2 * j + 2, 2 * j + 1, 2 * j, 1, top, wait)
        return emit(2 * j + 3, 2 * j + 2, 2 * j + 1, 0, top, True)

    top = body(0, top, wait=False)
    top = lax.fori_loop(1, n // 2 - 1, body, top)
    emit(None, n - 1, n - 2, 1, top, True)
    emit(None, None, n - 1, 0, None, False)
    store(0, n - 2).wait()
    store(1, n - 1).wait()


def forward(dims, q_rows, c_rows, pairs, before):
    chunks, groups, _ = dims
    lanes = q_rows.shape[2]
    length = sum(p.shape[1] for p in pairs)
    first, last = before is None, c_rows is not None
    args = [q_rows] + ([c_rows] if last else []) + pairs + ([] if first else list(before))
    size = chunks * lanes * length
    return pl.pallas_call(
        functools.partial(forward_kernel, dims, len(pairs), first, last),
        in_specs=[IN_VMEM] * len(args),
        out_specs=[IN_PLACE, IN_VMEM, IN_VMEM, IN_VMEM],
        out_shape=[
            jax.ShapeDtypeStruct((chunks, length, lanes), bf16),
            jax.ShapeDtypeStruct((chunks, lanes), f32),
            jax.ShapeDtypeStruct((3 if last else 2, chunks, lanes), f32),
            jax.ShapeDtypeStruct((chunks, HD, lanes), f32),
        ],
        scratch_shapes=[
            pltpu.VMEM((groups, length, 2 * HD), bf16),
            pltpu.VMEM((groups, HD + 16, length), bf16),
            pltpu.VMEM((length, lanes), f32),
            pltpu.VMEM((2, length, lanes), bf16),
            pltpu.SemaphoreType.DMA((2,)),
        ],
        compiler_params=pltpu.CompilerParams(vmem_limit_bytes=VMEM_BYTES),
        cost_estimate=pl.CostEstimate(flops=16 * size * HD, bytes_accessed=2 * size, transcendentals=size),
        name="forward",
    )(*args)


def rolled(rows, shift):
    count = rows.shape[0]
    shift = shift % count
    return rows if shift == 0 else jnp.concatenate([rows[count - shift :], rows[: count - shift]], axis=0)


def backward_kernel(dims, pieces, peers, first, last, *refs):
    chunks, groups, per_group = dims
    refs = list(refs)
    q_ref, c_ref = refs.pop(0), refs.pop(0)
    piece_refs = [refs.pop(0) for _ in range(pieces)]
    e_hbm, top_ref, own_ref = [refs.pop(0) for _ in range(3)]
    peer_refs = [refs.pop(0) for _ in range(peers)]
    acc_ref = refs.pop(0) if first else None
    past_dq = None if first else refs.pop(0)
    blocks = peers + 1
    ctx_outs = [refs.pop(0) for _ in range(blocks)] if first else None
    dq_outs = [refs.pop(0) for _ in range(blocks)] if last else [refs.pop(0)]
    dkv_ref = refs.pop(0)
    whole_ref, key_t, expo, score_grad, key_sum, value_sum, factor, delta, rows, sem, row_sem = refs
    kv_ref = gathered(piece_refs, whole_ref)
    length = kv_ref.shape[1]
    lanes = q_ref.shape[2]
    steps = length // KEY_ROWS
    heads = lanes // rows.shape[1]
    per_block = chunks // blocks
    pad = jnp.zeros((HD, lanes), bf16)

    def group_of(c):
        return (c // per_group) % groups

    def fetch(slot, c):
        return pltpu.make_async_copy(e_hbm.at[c], expo.at[slot], sem.at[slot])

    fetch(0, 0).start()
    fetch(1, 1).start()
    for g in range(groups):
        key_t[g] = kv_ref[g].T[:HD]
    key_sum[...] = jnp.zeros_like(key_sum)
    value_sum[...] = jnp.zeros_like(value_sum)

    stats = [[own_ref[i] for i in range(3)]]
    for r in range(1, blocks):
        stats.append([rolled(peer_refs[r - 1][i], r * per_block) for i in range(3)])
    top = functools.reduce(jnp.maximum, [s[0] for s in stats])
    shares = [jnp.exp(s[0] - top) for s in stats]
    total = sum(s[1] * w for s, w in zip(stats, shares))
    delta[...] = sum(s[2] * w for s, w in zip(stats, shares)) / total
    factor[0] = jnp.exp(top_ref[...] - top) / total
    if first:
        factor[1] = shares[0] / total

    def put_rows(c, value):
        flat = jnp.concatenate([value[:, h * rows.shape[1] : (h + 1) * rows.shape[1]] for h in range(heads)], axis=0)
        offset = pl.multiple_of((c % per_block) * heads * HD, heads * HD)
        rows[c // per_block, :, pl.ds(offset, heads * HD)] = flat.astype(bf16).T

    def send_rows(outs):
        copies = [pltpu.make_async_copy(rows.at[s], outs[s], row_sem.at[s]) for s in range(blocks)]
        for copy in copies:
            copy.start()
        for copy in copies:
            copy.wait()

    if first:

        def put_context(c, _):
            put_rows(c, acc_ref[c] * factor[1, pl.ds(c, 1)])
            return 0

        lax.fori_loop(0, chunks, put_context, 0)
        send_rows(ctx_outs)

    def emit(ca, cb, slot):
        if ca is not None:
            ga = group_of(ca)
            weights = jnp.concatenate([pad, c_ref[ca]], axis=0)
            fa, da = factor[0, pl.ds(ca, 1)], delta[pl.ds(ca, 1)]
            scaled_c = (c_ref[ca].astype(f32) * fa).astype(bf16)
            fetch(slot, ca).wait()
        if cb is not None:
            gb = group_of(cb)
            fb = factor[0, pl.ds(cb, 1)] * SCALE
            scaled_q = (q_ref[cb].astype(f32) * fb).astype(bf16)
            dq = None
        for k in range(steps):
            ks = slice(k * KEY_ROWS, (k + 1) * KEY_ROWS)
            if cb is not None:
                ds = score_grad[ks]
                part = jnp.dot(key_t[gb, :, ks], ds, preferred_element_type=f32)
                dq = part if dq is None else dq + part
                key_sum[gb, :, ks] += lax.dot_general(scaled_q, ds, NT, preferred_element_type=f32)
            if ca is not None:
                e = expo[slot, ks]
                prob_grad = jnp.dot(kv_ref[ga, ks], weights, preferred_element_type=f32)
                score_grad[ks] = (e.astype(f32) * (prob_grad - da)).astype(bf16)
                value_sum[ga, :, ks] += lax.dot_general(scaled_c, e, NT, preferred_element_type=f32)
        if cb is not None:
            dq = dq * fb
            if not first:
                dq = dq + past_dq[cb]
            if last:
                put_rows(cb, dq)
            else:
                dq_outs[0][cb] = dq

    n = chunks
    emit(0, None, 0)

    def body(j, _):
        @pl.when(2 * j + 2 < n)
        def _():
            fetch(0, 2 * j + 2).start()

        emit(2 * j + 1, 2 * j, 1)

        @pl.when(2 * j + 2 < n)
        def _():
            fetch(1, 2 * j + 3).start()
            emit(2 * j + 2, 2 * j + 1, 0)

        return 0

    lax.fori_loop(0, n // 2, body, 0)
    emit(None, n - 1, None)
    if last:
        send_rows(dq_outs)
    for g in range(groups):
        both = jnp.concatenate([key_sum[g], value_sum[g]], axis=0)
        dkv_ref[:, g * 2 * HD : (g + 1) * 2 * HD] = both.T.astype(dkv_ref.dtype)


def backward(dims, q_rows, c_rows, pairs, expo, top, own, peers, acc, past_dq, last, tokens):
    chunks, groups, _ = dims
    lanes = q_rows.shape[2]
    length = sum(p.shape[1] for p in pairs)
    first = past_dq is None
    blocks = len(peers) + 1
    width = chunks // blocks * (lanes // tokens) * HD
    args = [q_rows, c_rows, *pairs, expo, top, own, *peers] + [acc if first else past_dq]
    specs = [IN_VMEM] * len(args)
    specs[2 + len(pairs)] = IN_PLACE
    row_block = jax.ShapeDtypeStruct((tokens, width), bf16)
    outs, out_specs = [], []
    if first:
        outs += [row_block] * blocks
        out_specs += [IN_PLACE] * blocks
    if last:
        outs += [row_block] * blocks
        out_specs += [IN_PLACE] * blocks
    else:
        outs.append(jax.ShapeDtypeStruct((chunks, HD, lanes), f32))
        out_specs.append(IN_VMEM)
    outs.append(jax.ShapeDtypeStruct((length, groups * 2 * HD), f32 if last else bf16))
    out_specs.append(IN_VMEM)
    size = chunks * lanes * length
    results = list(
        pl.pallas_call(
            functools.partial(backward_kernel, dims, len(pairs), len(peers), first, last),
            in_specs=specs,
            out_specs=out_specs,
            out_shape=outs,
            scratch_shapes=[
                pltpu.VMEM((groups, length, 2 * HD), bf16),
                pltpu.VMEM((groups, HD, length), bf16),
                pltpu.VMEM((2, length, lanes), bf16),
                pltpu.VMEM((length, lanes), bf16),
                pltpu.VMEM((groups, HD, length), f32),
                pltpu.VMEM((groups, HD, length), f32),
                pltpu.VMEM((2, chunks, lanes), f32),
                pltpu.VMEM((chunks, lanes), f32),
                pltpu.VMEM((blocks, tokens, width), bf16),
                pltpu.SemaphoreType.DMA((2,)),
                pltpu.SemaphoreType.DMA((blocks,)),
            ],
            compiler_params=pltpu.CompilerParams(vmem_limit_bytes=VMEM_BYTES),
            cost_estimate=pl.CostEstimate(flops=24 * size * HD, bytes_accessed=2 * size, transcendentals=0),
            name="backward",
        )(*args)
    )
    context = [results.pop(0) for _ in range(blocks)] if first else None
    dq = [results.pop(0) for _ in range(blocks)] if last else results.pop(0)
    return context, dq, results.pop(0)


def on_device(halves, seqs, enc_states, norm_gain, kv_weight, queries, cotangent):
    tokens, width = queries.shape
    groups = kv_weight.shape[1] // (2 * HD)
    per_group_heads = width // (groups * HD)
    heads = min(per_group_heads, max(1, 512 // tokens))
    per_group = per_group_heads // heads
    chunks = halves * groups * per_group
    dims = (chunks, groups, per_group)

    def from_seq(x, shift):
        return lax.ppermute(x, "seq", [(i, (i + shift) % seqs) for i in range(seqs)])

    def from_half(x, shift):
        return lax.ppermute(x, "half", [(i, (i + shift) % halves) for i in range(halves)])

    q_blocks = [queries] + [from_half(queries, s) for s in range(1, halves)]
    c_blocks = [cotangent] + [from_half(cotangent, s) for s in range(1, halves)]
    own_pairs = project(enc_states, norm_gain, kv_weight)
    order = sorted(range(seqs), key=lambda s: min(s, seqs - s))
    pair_blocks = [[own_pairs]]
    for s in order[1:]:
        if seqs > 2 and 2 * s == seqs:
            low, high = pair_blocks[order.index(s - 1)][0], pair_blocks[order.index(s + 1)][0]
            middle = low.shape[1] // 2
            pair_blocks.append([from_seq(low[:, :middle], 1), from_seq(high[:, middle:], -1)])
        else:
            pair_blocks.append([from_seq(own_pairs, s)])
    q_rows = turn(q_blocks, heads)
    c_rows = turn(c_blocks, heads)

    expos, tops, before = [], [], None
    for i, pairs in enumerate(pair_blocks):
        expo, top, stats, acc = forward(dims, q_rows, c_rows if i == seqs - 1 else None, pairs, before)
        expos.append(expo)
        tops.append(top)
        before = (stats, acc)
    peers = [from_half(stats, r) for r in range(1, halves)]

    dq, sends, context_parts = None, [], None
    for i in reversed(range(seqs)):
        parts, dq, dkv = backward(
            dims, q_rows, c_rows, pair_blocks[i], expos[i], tops[i], stats, peers, acc, dq, i == 0, tokens
        )
        if parts is not None:
            context_parts = parts
        sends.append(dkv if i == 0 else from_seq(dkv, -order[i]))

    def home(parts):
        arrived = [parts[0]] + [from_half(parts[s], -s) for s in range(1, halves)]
        return sum(x.astype(f32) for x in arrived).astype(bf16)

    context = home(context_parts)
    d_queries = home(dq)
    d_pairs = sum(x.astype(f32) for x in sends).astype(bf16)
    return (context, d_queries, d_pairs)


def solution(mesh):
    shape = mesh.shape
    rows, columns = P(("half", "seq"), None), P(("half", "seq"), "head")

    def body(*args):
        return on_device(shape["half"], shape["seq"], *args)

    return jax.shard_map(
        body,
        mesh=mesh,
        in_specs=(rows, P(), P(None, "head"), columns, columns),
        out_specs=(columns, columns, columns),
        check_vma=False,
    )
```

```python
import functools
import math

import jax
import jax.numpy as jnp
from jax import lax
from jax.experimental import pallas as pl
from jax.experimental.pallas import tpu as pltpu
from jax.sharding import PartitionSpec as P


HD = 64
EPS = 1e-06
LOG2E = math.log2(math.e)
SCALE = HD ** (-0.5)
KEY_ROWS = 256
VMEM_BYTES = 14 << 20
NT = (((1,), (1,)), ((), ()))

bf16 = jnp.bfloat16
f32 = jnp.float32

IN_VMEM = pl.BlockSpec(memory_space=pltpu.VMEM)
IN_PLACE = pl.BlockSpec(memory_space=pl.ANY)


def project_kernel(x_ref, gain_ref, w_ref, out_ref):
    x = x_ref[...].astype(f32)
    inverse_root = lax.rsqrt(jnp.mean(x * x, axis=1, keepdims=True) + EPS)
    normed = (x * inverse_root * gain_ref[...]).astype(bf16)
    pairs = jnp.dot(normed, w_ref[...], preferred_element_type=f32).astype(bf16)
    for g in range(out_ref.shape[0]):
        out_ref[g] = pairs[:, g * 2 * HD : (g + 1) * 2 * HD]


def project(states, gain, weight):
    rows, width = states.shape
    groups = weight.shape[1] // (2 * HD)
    block = min(rows, 256)
    return pl.pallas_call(
        project_kernel,
        grid=(rows // block,),
        in_specs=[
            pl.BlockSpec((block, width), lambda i: (i, 0)),
            pl.BlockSpec((1, width), lambda i: (0, 0)),
            pl.BlockSpec((width, weight.shape[1]), lambda i: (0, 0)),
        ],
        out_specs=pl.BlockSpec((groups, block, 2 * HD), lambda i: (0, i, 0)),
        out_shape=jax.ShapeDtypeStruct((groups, rows, 2 * HD), bf16),
        compiler_params=pltpu.CompilerParams(vmem_limit_bytes=60 << 20),
        cost_estimate=pl.CostEstimate(
            flops=2 * rows * width * weight.shape[1], bytes_accessed=2 * rows * width, transcendentals=0
        ),
        name="project",
    )(states, gain.reshape(1, width), weight)


def turn_kernel(count, *refs):
    inputs, out_ref = refs[:count], refs[count]
    chunks, _, lanes = out_ref.shape
    per_block = chunks // count
    tokens = inputs[0].shape[0]
    heads = lanes // tokens
    for s in range(count):
        turned = inputs[s][...].T
        for i in range(per_block):
            base = i * heads * HD
            out_ref[s * per_block + i] = jnp.concatenate(
                [turned[base + h * HD : base + (h + 1) * HD] for h in range(heads)], axis=1
            )


def turn(blocks, heads):
    tokens, width = blocks[0].shape
    chunks = len(blocks) * width // (heads * HD)
    return pl.pallas_call(
        functools.partial(turn_kernel, len(blocks)),
        in_specs=[IN_VMEM] * len(blocks),
        out_specs=IN_VMEM,
        out_shape=jax.ShapeDtypeStruct((chunks, HD, heads * tokens), bf16),
        compiler_params=pltpu.CompilerParams(vmem_limit_bytes=VMEM_BYTES),
        name="turn",
    )(*blocks)


def gathered(piece_refs, whole_ref):
    if len(piece_refs) == 1:
        return piece_refs[0]
    begin = 0
    for piece in piece_refs:
        rows = piece.shape[1]
        whole_ref[:, begin : begin + rows] = piece[...]
        begin += rows
    return whole_ref


def forward_kernel(dims, pieces, first, last, *refs):
    chunks, groups, per_group = dims
    refs = list(refs)
    q_ref = refs.pop(0)
    c_ref = refs.pop(0) if last else None
    piece_refs = [refs.pop(0) for _ in range(pieces)]
    past, past_acc = (None, None) if first else (refs.pop(0), refs.pop(0))
    e_hbm, top_ref, st_ref, acc_ref, whole_ref, value_t, scores, expo, sem = refs
    kv_ref = gathered(piece_refs, whole_ref)
    length = kv_ref.shape[1]
    lanes = q_ref.shape[2]
    pad = jnp.zeros((HD, lanes), bf16)
    steps = length // KEY_ROWS
    for g in range(groups):
        value_t[g, :HD] = kv_ref[g].T[HD:]
        value_t[g, HD:] = jnp.ones((16, length), bf16)

    def group_of(c):
        return (c // per_group) % groups

    def store(slot, c):
        return pltpu.make_async_copy(expo.at[slot], e_hbm.at[c], sem.at[slot])

    def emit(ca, cb, cc, slot, top, wait):
        largest, total = None, None
        if ca is not None:
            weights = jnp.concatenate([q_ref[ca] * jnp.asarray(SCALE, bf16), pad], axis=0)
            ga = group_of(ca)
        if cb is not None:
            low_top = top * LOG2E
            if wait:
                store(slot, cb).wait()
        if cc is not None:
            gc = group_of(cc)
        for k in range(steps):
            ks = slice(k * KEY_ROWS, (k + 1) * KEY_ROWS)
            if cb is not None:
                expo[slot, ks] = jnp.exp2(scores[ks] * LOG2E - low_top).astype(bf16)
            if ca is not None:
                s = jnp.dot(kv_ref[ga, ks], weights, preferred_element_type=f32)
                scores[ks] = s
                part = jnp.max(s.reshape(KEY_ROWS // 8, 8, lanes), axis=0)
                largest = part if largest is None else jnp.maximum(largest, part)
            if cc is not None:
                part = jnp.dot(value_t[gc, :, ks], expo[1 - slot, ks], preferred_element_type=f32)
                total = part if total is None else total + part
        if cb is not None:
            top_ref[pl.ds(cb, 1)] = top
            store(slot, cb).start()
        if cc is not None:
            m = top_ref[pl.ds(cc, 1)]
            l = total[HD : HD + 1]
            acc = total[:HD]
            if not first:
                before = past[0, pl.ds(cc, 1)]
                both = jnp.maximum(before, m)
                old, new = jnp.exp(before - both), jnp.exp(m - both)
                l = past[1, pl.ds(cc, 1)] * old + l * new
                acc = past_acc[cc] * old + acc * new
                m = both
            st_ref[0, pl.ds(cc, 1)] = m
            st_ref[1, pl.ds(cc, 1)] = l
            if last:
                st_ref[2, pl.ds(cc, 1)] = jnp.sum(c_ref[cc].astype(f32) * acc, axis=0, keepdims=True)
            acc_ref[cc] = acc
        return None if largest is None else jnp.max(largest, axis=0, keepdims=True)

    n = chunks
    top = emit(0, None, None, None, None, False)
    top = emit(1, 0, None, 0, top, False)

    def body(j, top, wait=True):
        top = emit(2 * j + 2, 2 * j + 1, 2 * j, 1, top, wait)
        return emit(2 * j + 3, 2 * j + 2, 2 * j + 1, 0, top, True)

    top = body(0, top, wait=False)
    top = lax.fori_loop(1, n // 2 - 1, body, top)
    emit(None, n - 1, n - 2, 1, top, True)
    emit(None, None, n - 1, 0, None, False)
    store(0, n - 2).wait()
    store(1, n - 1).wait()


def forward(dims, q_rows, c_rows, pairs, before):
    chunks, groups, _ = dims
    lanes = q_rows.shape[2]
    length = sum(p.shape[1] for p in pairs)
    first, last = before is None, c_rows is not None
    args = [q_rows] + ([c_rows] if last else []) + pairs + ([] if first else list(before))
    size = chunks * lanes * length
    return pl.pallas_call(
        functools.partial(forward_kernel, dims, len(pairs), first, last),
        in_specs=[IN_VMEM] * len(args),
        out_specs=[IN_PLACE, IN_VMEM, IN_VMEM, IN_VMEM],
        out_shape=[
            jax.ShapeDtypeStruct((chunks, length, lanes), bf16),
            jax.ShapeDtypeStruct((chunks, lanes), f32),
            jax.ShapeDtypeStruct((3 if last else 2, chunks, lanes), f32),
            jax.ShapeDtypeStruct((chunks, HD, lanes), f32),
        ],
        scratch_shapes=[
            pltpu.VMEM((groups, length, 2 * HD), bf16),
            pltpu.VMEM((groups, HD + 16, length), bf16),
            pltpu.VMEM((length, lanes), f32),
            pltpu.VMEM((2, length, lanes), bf16),
            pltpu.SemaphoreType.DMA((2,)),
        ],
        compiler_params=pltpu.CompilerParams(vmem_limit_bytes=VMEM_BYTES),
        cost_estimate=pl.CostEstimate(flops=16 * size * HD, bytes_accessed=2 * size, transcendentals=size),
        name="forward",
    )(*args)


def rolled(rows, shift):
    count = rows.shape[0]
    shift = shift % count
    return rows if shift == 0 else jnp.concatenate([rows[count - shift :], rows[: count - shift]], axis=0)


def backward_kernel(dims, pieces, peers, first, last, *refs):
    chunks, groups, per_group = dims
    refs = list(refs)
    q_ref, c_ref = refs.pop(0), refs.pop(0)
    piece_refs = [refs.pop(0) for _ in range(pieces)]
    e_hbm, top_ref, own_ref = [refs.pop(0) for _ in range(3)]
    peer_refs = [refs.pop(0) for _ in range(peers)]
    acc_ref = refs.pop(0) if first else None
    past_dq = None if first else refs.pop(0)
    blocks = peers + 1
    ctx_outs = [refs.pop(0) for _ in range(blocks)] if first else None
    dq_outs = [refs.pop(0) for _ in range(blocks)] if last else [refs.pop(0)]
    dkv_ref = refs.pop(0)
    whole_ref, key_t, expo, score_grad, key_sum, value_sum, factor, delta, rows, sem, row_sem = refs
    kv_ref = gathered(piece_refs, whole_ref)
    length = kv_ref.shape[1]
    lanes = q_ref.shape[2]
    steps = length // KEY_ROWS
    heads = lanes // rows.shape[1]
    per_block = chunks // blocks
    pad = jnp.zeros((HD, lanes), bf16)

    def group_of(c):
        return (c // per_group) % groups

    def fetch(slot, c):
        return pltpu.make_async_copy(e_hbm.at[c], expo.at[slot], sem.at[slot])

    fetch(0, 0).start()
    fetch(1, 1).start()
    for g in range(groups):
        key_t[g] = kv_ref[g].T[:HD]
    key_sum[...] = jnp.zeros_like(key_sum)
    value_sum[...] = jnp.zeros_like(value_sum)

    stats = [[own_ref[i] for i in range(3)]]
    for r in range(1, blocks):
        stats.append([rolled(peer_refs[r - 1][i], r * per_block) for i in range(3)])
    top = functools.reduce(jnp.maximum, [s[0] for s in stats])
    shares = [jnp.exp(s[0] - top) for s in stats]
    total = sum(s[1] * w for s, w in zip(stats, shares))
    delta[...] = sum(s[2] * w for s, w in zip(stats, shares)) / total
    factor[0] = jnp.exp(top_ref[...] - top) / total
    if first:
        factor[1] = shares[0] / total

    def put_rows(c, value):
        flat = jnp.concatenate([value[:, h * rows.shape[1] : (h + 1) * rows.shape[1]] for h in range(heads)], axis=0)
        offset = pl.multiple_of((c % per_block) * heads * HD, heads * HD)
        rows[c // per_block, :, pl.ds(offset, heads * HD)] = flat.astype(bf16).T

    def send_rows(outs):
        copies = [pltpu.make_async_copy(rows.at[s], outs[s], row_sem.at[s]) for s in range(blocks)]
        for copy in copies:
            copy.start()
        for copy in copies:
            copy.wait()

    if first:

        def put_context(c, _):
            put_rows(c, acc_ref[c] * factor[1, pl.ds(c, 1)])
            return 0

        lax.fori_loop(0, chunks, put_context, 0)
        send_rows(ctx_outs)

    def emit(ca, cb, slot):
        if ca is not None:
            ga = group_of(ca)
            weights = jnp.concatenate([pad, c_ref[ca]], axis=0)
            fa, da = factor[0, pl.ds(ca, 1)], delta[pl.ds(ca, 1)]
            scaled_c = (c_ref[ca].astype(f32) * fa).astype(bf16)
            fetch(slot, ca).wait()
        if cb is not None:
            gb = group_of(cb)
            fb = factor[0, pl.ds(cb, 1)] * SCALE
            scaled_q = (q_ref[cb].astype(f32) * fb).astype(bf16)
            dq = None
        for k in range(steps):
            ks = slice(k * KEY_ROWS, (k + 1) * KEY_ROWS)
            if cb is not None:
                ds = score_grad[ks]
                part = jnp.dot(key_t[gb, :, ks], ds, preferred_element_type=f32)
                dq = part if dq is None else dq + part
                key_sum[gb, :, ks] += lax.dot_general(scaled_q, ds, NT, preferred_element_type=f32)
            if ca is not None:
                e = expo[slot, ks]
                prob_grad = jnp.dot(kv_ref[ga, ks], weights, preferred_element_type=f32)
                score_grad[ks] = (e.astype(f32) * (prob_grad - da)).astype(bf16)
                value_sum[ga, :, ks] += lax.dot_general(scaled_c, e, NT, preferred_element_type=f32)
        if cb is not None:
            dq = dq * fb
            if not first:
                dq = dq + past_dq[cb]
            if last:
                put_rows(cb, dq)
            else:
                dq_outs[0][cb] = dq

    n = chunks
    emit(0, None, 0)

    def body(j, _):
        @pl.when(2 * j + 2 < n)
        def _():
            fetch(0, 2 * j + 2).start()

        emit(2 * j + 1, 2 * j, 1)

        @pl.when(2 * j + 2 < n)
        def _():
            fetch(1, 2 * j + 3).start()
            emit(2 * j + 2, 2 * j + 1, 0)

        return 0

    lax.fori_loop(0, n // 2, body, 0)
    emit(None, n - 1, None)
    if last:
        send_rows(dq_outs)
    for g in range(groups):
        both = jnp.concatenate([key_sum[g], value_sum[g]], axis=0)
        dkv_ref[:, g * 2 * HD : (g + 1) * 2 * HD] = both.T.astype(dkv_ref.dtype)


def backward(dims, q_rows, c_rows, pairs, expo, top, own, peers, acc, past_dq, last, tokens):
    chunks, groups, _ = dims
    lanes = q_rows.shape[2]
    length = sum(p.shape[1] for p in pairs)
    first = past_dq is None
    blocks = len(peers) + 1
    width = chunks // blocks * (lanes // tokens) * HD
    args = [q_rows, c_rows, *pairs, expo, top, own, *peers] + [acc if first else past_dq]
    specs = [IN_VMEM] * len(args)
    specs[2 + len(pairs)] = IN_PLACE
    row_block = jax.ShapeDtypeStruct((tokens, width), bf16)
    outs, out_specs = [], []
    if first:
        outs += [row_block] * blocks
        out_specs += [IN_PLACE] * blocks
    if last:
        outs += [row_block] * blocks
        out_specs += [IN_PLACE] * blocks
    else:
        outs.append(jax.ShapeDtypeStruct((chunks, HD, lanes), f32))
        out_specs.append(IN_VMEM)
    outs.append(jax.ShapeDtypeStruct((length, groups * 2 * HD), f32 if last else bf16))
    out_specs.append(IN_VMEM)
    size = chunks * lanes * length
    results = list(
        pl.pallas_call(
            functools.partial(backward_kernel, dims, len(pairs), len(peers), first, last),
            in_specs=specs,
            out_specs=out_specs,
            out_shape=outs,
            scratch_shapes=[
                pltpu.VMEM((groups, length, 2 * HD), bf16),
                pltpu.VMEM((groups, HD, length), bf16),
                pltpu.VMEM((2, length, lanes), bf16),
                pltpu.VMEM((length, lanes), bf16),
                pltpu.VMEM((groups, HD, length), f32),
                pltpu.VMEM((groups, HD, length), f32),
                pltpu.VMEM((2, chunks, lanes), f32),
                pltpu.VMEM((chunks, lanes), f32),
                pltpu.VMEM((blocks, tokens, width), bf16),
                pltpu.SemaphoreType.DMA((2,)),
                pltpu.SemaphoreType.DMA((blocks,)),
            ],
            compiler_params=pltpu.CompilerParams(vmem_limit_bytes=VMEM_BYTES),
            cost_estimate=pl.CostEstimate(flops=24 * size * HD, bytes_accessed=2 * size, transcendentals=0),
            name="backward",
        )(*args)
    )
    context = [results.pop(0) for _ in range(blocks)] if first else None
    dq = [results.pop(0) for _ in range(blocks)] if last else results.pop(0)
    return context, dq, results.pop(0)


def on_device(halves, seqs, enc_states, norm_gain, kv_weight, queries, cotangent):
    tokens, width = queries.shape
    groups = kv_weight.shape[1] // (2 * HD)
    per_group_heads = width // (groups * HD)
    heads = min(per_group_heads, max(1, 512 // tokens))
    per_group = per_group_heads // heads
    chunks = seqs // max(1, seqs // 2) * groups * per_group
    dims = (chunks, groups, per_group)

    near = max(1, seqs // 2)
    fars = seqs // near

    def from_far(x, shift):
        return lax.ppermute(x, "seq", [(i, (i + shift * near) % seqs) for i in range(seqs)])

    def from_near(x, a, b):
        pairs = []
        for h in range(halves):
            for i in range(seqs):
                to = (h + a) % halves * seqs + i // near * near + (i + b) % near
                pairs.append((h * seqs + i, to))
        return lax.ppermute(x, ("half", "seq"), pairs)

    q_blocks = [queries] + [from_far(queries, s) for s in range(1, fars)]
    late, *_ = lax.optimization_barrier((cotangent, *q_blocks[1:]))
    c_blocks = [late] + [from_far(late, s) for s in range(1, fars)]
    own_pairs = project(enc_states, norm_gain, kv_weight)
    order = sorted(
        ((a, b) for a in range(halves) for b in range(near)), key=lambda s: (s != (0, 0), s[0] > 0 and s[1] > 0)
    )
    blocks = {(0, 0): [own_pairs]}
    for a, b in order[1:]:
        if a and b:
            across, along = blocks[a, 0][0], blocks[0, b][0]
            middle = across.shape[1] // 2
            blocks[a, b] = [from_near(along[:, :middle], a, 0), from_near(across[:, middle:], 0, b)]
        else:
            blocks[a, b] = [from_near(own_pairs, a, b)]
    pair_blocks = [blocks[s] for s in order]
    count = len(order)
    q_rows = turn(q_blocks, heads)
    c_rows = turn(c_blocks, heads)

    expos, tops, before = [], [], None
    for i, pairs in enumerate(pair_blocks):
        expo, top, stats, acc = forward(dims, q_rows, c_rows if i == count - 1 else None, pairs, before)
        expos.append(expo)
        tops.append(top)
        before = (stats, acc)
    peers = [from_far(stats, r) for r in range(1, fars)]

    dq, sends, context_parts = None, [], None
    for i in reversed(range(count)):
        parts, dq, dkv = backward(
            dims, q_rows, c_rows, pair_blocks[i], expos[i], tops[i], stats, peers, acc, dq, i == 0, tokens
        )
        if parts is not None:
            context_parts = parts
        sends.append(dkv if i == 0 else from_near(dkv, -order[i][0], -order[i][1]))

    def home(parts):
        arrived = [parts[0]] + [from_far(parts[s], -s) for s in range(1, fars)]
        return sum(x.astype(f32) for x in arrived).astype(bf16)

    context = home(context_parts)
    d_queries = home(dq)
    d_pairs = sum(x.astype(f32) for x in sends).astype(bf16)
    return (context, d_queries, d_pairs)


def solution(mesh):
    shape = mesh.shape
    rows, columns = P(("half", "seq"), None), P(("half", "seq"), "head")

    def body(*args):
        return on_device(shape["half"], shape["seq"], *args)

    return jax.shard_map(
        body,
        mesh=mesh,
        in_specs=(rows, P(), P(None, "head"), columns, columns),
        out_specs=(columns, columns, columns),
        check_vma=False,
    )
```

```python
import functools
import math

import jax
import jax.numpy as jnp
from jax import lax
from jax.experimental import pallas as pl
from jax.experimental.pallas import tpu as pltpu
from jax.sharding import PartitionSpec as P


HD = 64
EPS = 1e-06
LOG2E = math.log2(math.e)
SCALE = HD ** (-0.5)
KEY_ROWS = 256
VMEM_BYTES = 14 << 20
NT = (((1,), (1,)), ((), ()))

bf16 = jnp.bfloat16
f32 = jnp.float32

IN_VMEM = pl.BlockSpec(memory_space=pltpu.VMEM)
IN_PLACE = pl.BlockSpec(memory_space=pl.ANY)


def project_kernel(x_ref, gain_ref, w_ref, out_ref):
    x = x_ref[...].astype(f32)
    inverse_root = lax.rsqrt(jnp.mean(x * x, axis=1, keepdims=True) + EPS)
    normed = (x * inverse_root * gain_ref[...]).astype(bf16)
    pairs = jnp.dot(normed, w_ref[...], preferred_element_type=f32).astype(bf16)
    for g in range(out_ref.shape[0]):
        out_ref[g] = pairs[:, g * 2 * HD : (g + 1) * 2 * HD]


def project(states, gain, weight):
    rows, width = states.shape
    groups = weight.shape[1] // (2 * HD)
    block = min(rows, 256)
    return pl.pallas_call(
        project_kernel,
        grid=(rows // block,),
        in_specs=[
            pl.BlockSpec((block, width), lambda i: (i, 0)),
            pl.BlockSpec((1, width), lambda i: (0, 0)),
            pl.BlockSpec((width, weight.shape[1]), lambda i: (0, 0)),
        ],
        out_specs=pl.BlockSpec((groups, block, 2 * HD), lambda i: (0, i, 0)),
        out_shape=jax.ShapeDtypeStruct((groups, rows, 2 * HD), bf16),
        compiler_params=pltpu.CompilerParams(vmem_limit_bytes=60 << 20),
        cost_estimate=pl.CostEstimate(
            flops=2 * rows * width * weight.shape[1], bytes_accessed=2 * rows * width, transcendentals=0
        ),
        name="project",
    )(states, gain.reshape(1, width), weight)


def turn_kernel(count, *refs):
    inputs, out_ref = refs[:count], refs[count]
    chunks, _, lanes = out_ref.shape
    per_block = chunks // count
    tokens = inputs[0].shape[0]
    heads = lanes // tokens
    for s in range(count):
        turned = inputs[s][...].T
        for i in range(per_block):
            base = i * heads * HD
            out_ref[s * per_block + i] = jnp.concatenate(
                [turned[base + h * HD : base + (h + 1) * HD] for h in range(heads)], axis=1
            )


def turn(blocks, heads):
    tokens, width = blocks[0].shape
    chunks = len(blocks) * width // (heads * HD)
    return pl.pallas_call(
        functools.partial(turn_kernel, len(blocks)),
        in_specs=[IN_VMEM] * len(blocks),
        out_specs=IN_VMEM,
        out_shape=jax.ShapeDtypeStruct((chunks, HD, heads * tokens), bf16),
        compiler_params=pltpu.CompilerParams(vmem_limit_bytes=VMEM_BYTES),
        name="turn",
    )(*blocks)


def gathered(piece_refs, whole_ref):
    if len(piece_refs) == 1:
        return piece_refs[0]
    begin = 0
    for piece in piece_refs:
        rows = piece.shape[1]
        whole_ref[:, begin : begin + rows] = piece[...]
        begin += rows
    return whole_ref


def forward_kernel(dims, pieces, first, last, *refs):
    chunks, groups, per_group = dims
    refs = list(refs)
    q_ref = refs.pop(0)
    c_ref = refs.pop(0) if last else None
    piece_refs = [refs.pop(0) for _ in range(pieces)]
    past, past_acc = (None, None) if first else (refs.pop(0), refs.pop(0))
    e_ref, top_ref, st_ref, acc_ref, whole_ref, value_t, scores, expo = refs
    kv_ref = gathered(piece_refs, whole_ref)
    length = kv_ref.shape[1]
    lanes = q_ref.shape[2]
    pad = jnp.zeros((HD, lanes), bf16)
    steps = length // KEY_ROWS
    for g in range(groups):
        value_t[g, :HD] = kv_ref[g].T[HD:]
        value_t[g, HD:] = jnp.ones((16, length), bf16)

    def group_of(c):
        return (c // per_group) % groups

    def emit(ca, cb, cc, slot, top):
        largest, total = None, None
        if ca is not None:
            weights = jnp.concatenate([q_ref[ca] * jnp.asarray(SCALE, bf16), pad], axis=0)
            ga = group_of(ca)
        if cb is not None:
            low_top = top * LOG2E
        if cc is not None:
            gc = group_of(cc)
        for k in range(steps):
            ks = slice(k * KEY_ROWS, (k + 1) * KEY_ROWS)
            if cb is not None:
                weight = jnp.exp2(scores[ks] * LOG2E - low_top).astype(bf16)
                expo[slot, ks] = weight
                e_ref[cb, ks] = weight
            if ca is not None:
                s = jnp.dot(kv_ref[ga, ks], weights, preferred_element_type=f32)
                scores[ks] = s
                part = jnp.max(s.reshape(KEY_ROWS // 8, 8, lanes), axis=0)
                largest = part if largest is None else jnp.maximum(largest, part)
            if cc is not None:
                part = jnp.dot(value_t[gc, :, ks], expo[1 - slot, ks], preferred_element_type=f32)
                total = part if total is None else total + part
        if cb is not None:
            top_ref[pl.ds(cb, 1)] = top
        if cc is not None:
            m = top_ref[pl.ds(cc, 1)]
            l = total[HD : HD + 1]
            acc = total[:HD]
            if not first:
                before = past[0, pl.ds(cc, 1)]
                both = jnp.maximum(before, m)
                old, new = jnp.exp(before - both), jnp.exp(m - both)
                l = past[1, pl.ds(cc, 1)] * old + l * new
                acc = past_acc[cc] * old + acc * new
                m = both
            st_ref[0, pl.ds(cc, 1)] = m
            st_ref[1, pl.ds(cc, 1)] = l
            if last:
                st_ref[2, pl.ds(cc, 1)] = jnp.sum(c_ref[cc].astype(f32) * acc, axis=0, keepdims=True)
            acc_ref[cc] = acc
        return None if largest is None else jnp.max(largest, axis=0, keepdims=True)

    n = chunks
    top = emit(0, None, None, None, None)
    top = emit(1, 0, None, 0, top)

    def body(j, top):
        top = emit(2 * j + 2, 2 * j + 1, 2 * j, 1, top)
        return emit(2 * j + 3, 2 * j + 2, 2 * j + 1, 0, top)

    top = lax.fori_loop(0, n // 2 - 1, body, top)
    emit(None, n - 1, n - 2, 1, top)
    emit(None, None, n - 1, 0, None)


def forward(dims, q_rows, c_rows, pairs, before):
    chunks, groups, _ = dims
    lanes = q_rows.shape[2]
    length = sum(p.shape[1] for p in pairs)
    first, last = before is None, c_rows is not None
    args = [q_rows] + ([c_rows] if last else []) + pairs + ([] if first else list(before))
    size = chunks * lanes * length
    return pl.pallas_call(
        functools.partial(forward_kernel, dims, len(pairs), first, last),
        in_specs=[IN_VMEM] * len(args),
        out_specs=[IN_VMEM] * 4,
        out_shape=[
            jax.ShapeDtypeStruct((chunks, length, lanes), bf16),
            jax.ShapeDtypeStruct((chunks, lanes), f32),
            jax.ShapeDtypeStruct((3 if last else 2, chunks, lanes), f32),
            jax.ShapeDtypeStruct((chunks, HD, lanes), f32),
        ],
        scratch_shapes=[
            pltpu.VMEM((groups, length, 2 * HD), bf16),
            pltpu.VMEM((groups, HD + 16, length), bf16),
            pltpu.VMEM((length, lanes), f32),
            pltpu.VMEM((2, length, lanes), bf16),
        ],
        compiler_params=pltpu.CompilerParams(vmem_limit_bytes=VMEM_BYTES),
        cost_estimate=pl.CostEstimate(flops=16 * size * HD, bytes_accessed=2 * size, transcendentals=size),
        name="forward",
    )(*args)


def rolled(rows, shift):
    count = rows.shape[0]
    shift = shift % count
    return rows if shift == 0 else jnp.concatenate([rows[count - shift :], rows[: count - shift]], axis=0)


def backward_kernel(dims, pieces, peers, span, first, last, *refs):
    chunks, groups, per_group = dims
    begin, end = span
    blocks = peers + 1
    per_block = chunks // blocks
    whole_span = span == (0, chunks)
    refs = list(refs)
    q_ref, c_ref = refs.pop(0), refs.pop(0)
    piece_refs = [refs.pop(0) for _ in range(pieces)]
    e_ref, top_ref, own_ref = [refs.pop(0) for _ in range(3)]
    peer_refs = [refs.pop(0) for _ in range(peers)]
    acc_ref = refs.pop(0) if first else None
    past_dq = None if first else refs.pop(0)
    past_sums = [refs.pop(0), refs.pop(0)] if begin == 0 and not whole_span else None
    ctx_outs = [refs.pop(0) for _ in range(blocks)] if first else None
    sent = list(range(begin // per_block, end // per_block))
    dq_outs = [refs.pop(0) for _ in sent] if last else [refs.pop(0)]
    outs = [refs.pop(0)] if begin == 0 else [refs.pop(0), refs.pop(0)]
    whole_ref, key_t, score_grad, key_sum, value_sum, factor, delta, rows, row_sem = refs
    kv_ref = gathered(piece_refs, whole_ref)
    length = kv_ref.shape[1]
    lanes = q_ref.shape[2]
    steps = length // KEY_ROWS
    tokens = rows.shape[1]
    heads = lanes // tokens
    pad = jnp.zeros((HD, lanes), bf16)

    def group_of(c):
        return (c // per_group) % groups

    for g in range(groups):
        key_t[g] = kv_ref[g].T[:HD]
    key_sum[...] = jnp.zeros_like(key_sum) if past_sums is None else past_sums[0][...]
    value_sum[...] = jnp.zeros_like(value_sum) if past_sums is None else past_sums[1][...]

    stats = [[own_ref[i] for i in range(3)]]
    for r in range(1, blocks):
        stats.append([rolled(peer_refs[r - 1][i], r * per_block) for i in range(3)])
    top = functools.reduce(jnp.maximum, [s[0] for s in stats])
    shares = [jnp.exp(s[0] - top) for s in stats]
    total = sum(s[1] * w for s, w in zip(stats, shares))
    delta[...] = sum(s[2] * w for s, w in zip(stats, shares)) / total
    factor[0] = jnp.exp(top_ref[...] - top) / total
    if first:
        factor[1] = shares[0] / total

    def put_rows(c, value):
        flat = jnp.concatenate([value[:, h * tokens : (h + 1) * tokens] for h in range(heads)], axis=0)
        offset = pl.multiple_of((c % per_block) * heads * HD, heads * HD)
        rows[c // per_block, :, pl.ds(offset, heads * HD)] = flat.astype(bf16).T

    def send_rows(which, refs):
        copies = [pltpu.make_async_copy(rows.at[s], ref, row_sem.at[s]) for s, ref in zip(which, refs)]
        for copy in copies:
            copy.start()
        for copy in copies:
            copy.wait()

    if first:

        def put_context(c, _):
            put_rows(c, acc_ref[c] * factor[1, pl.ds(c, 1)])
            return 0

        lax.fori_loop(0, chunks, put_context, 0)
        send_rows(range(blocks), ctx_outs)

    def emit(ca, cb):
        if ca is not None:
            ga = group_of(ca)
            weights = jnp.concatenate([pad, c_ref[ca]], axis=0)
            fa, da = factor[0, pl.ds(ca, 1)], delta[pl.ds(ca, 1)]
            scaled_c = (c_ref[ca].astype(f32) * fa).astype(bf16)
        if cb is not None:
            gb = group_of(cb)
            fb = factor[0, pl.ds(cb, 1)] * SCALE
            scaled_q = (q_ref[cb].astype(f32) * fb).astype(bf16)
            dq = None
        for k in range(steps):
            ks = slice(k * KEY_ROWS, (k + 1) * KEY_ROWS)
            if cb is not None:
                ds = score_grad[ks]
                part = jnp.dot(key_t[gb, :, ks], ds, preferred_element_type=f32)
                dq = part if dq is None else dq + part
                key_sum[gb, :, ks] += lax.dot_general(scaled_q, ds, NT, preferred_element_type=f32)
            if ca is not None:
                e = e_ref[ca, ks]
                prob_grad = jnp.dot(kv_ref[ga, ks], weights, preferred_element_type=f32)
                score_grad[ks] = (e.astype(f32) * (prob_grad - da)).astype(bf16)
                value_sum[ga, :, ks] += lax.dot_general(scaled_c, e, NT, preferred_element_type=f32)
        if cb is not None:
            dq = dq * fb
            if not first:
                dq = dq + past_dq[cb]
            if last:
                put_rows(cb, dq)
            else:
                dq_outs[0][cb] = dq

    emit(begin, None)

    def body(j, _):
        c = begin + 2 * j
        emit(c + 1, c)
        emit(c + 2, c + 1)
        return 0

    lax.fori_loop(0, (end - begin) // 2 - 1, body, 0)
    emit(end - 1, end - 2)
    emit(None, end - 1)
    if last:
        send_rows(sent, dq_outs)
    if begin > 0:
        outs[0][...] = key_sum[...]
        outs[1][...] = value_sum[...]
    else:
        for g in range(groups):
            both = jnp.concatenate([key_sum[g].astype(bf16), value_sum[g].astype(bf16)], axis=0)
            outs[0][:, g * 2 * HD : (g + 1) * 2 * HD] = both.T


def backward(dims, q_rows, c_rows, pairs, expo, top, own, peers, acc, past_dq, past_sums, span, last, tokens):
    chunks, groups, _ = dims
    begin, end = span
    lanes = q_rows.shape[2]
    length = sum(p.shape[1] for p in pairs)
    first = past_dq is None
    blocks = len(peers) + 1
    per_block = chunks // blocks
    width = per_block * (lanes // tokens) * HD
    args = [q_rows, c_rows, *pairs, expo, top, own, *peers] + [acc if first else past_dq] + list(past_sums or [])
    row_block = jax.ShapeDtypeStruct((tokens, width), bf16)
    sums = jax.ShapeDtypeStruct((groups, HD, length), f32)
    outs, out_specs = [], []
    if first:
        outs += [row_block] * blocks
        out_specs += [IN_PLACE] * blocks
    sent = (end - begin) // per_block
    if last:
        outs += [row_block] * sent
        out_specs += [IN_PLACE] * sent
    else:
        outs.append(jax.ShapeDtypeStruct((chunks, HD, lanes), f32))
        out_specs.append(IN_VMEM)
    if begin > 0:
        outs += [sums] * 2
        out_specs += [IN_VMEM] * 2
    else:
        outs.append(jax.ShapeDtypeStruct((length, groups * 2 * HD), bf16))
        out_specs.append(IN_VMEM)
    size = (end - begin) * lanes * length
    results = list(
        pl.pallas_call(
            functools.partial(backward_kernel, dims, len(pairs), len(peers), span, first, last),
            in_specs=[IN_VMEM] * len(args),
            out_specs=out_specs,
            out_shape=outs,
            scratch_shapes=[
                pltpu.VMEM((groups, length, 2 * HD), bf16),
                pltpu.VMEM((groups, HD, length), bf16),
                pltpu.VMEM((length, lanes), bf16),
                pltpu.VMEM((groups, HD, length), f32),
                pltpu.VMEM((groups, HD, length), f32),
                pltpu.VMEM((2, chunks, lanes), f32),
                pltpu.VMEM((chunks, lanes), f32),
                pltpu.VMEM((blocks, tokens, width), bf16),
                pltpu.SemaphoreType.DMA((blocks,)),
            ],
            compiler_params=pltpu.CompilerParams(vmem_limit_bytes=VMEM_BYTES),
            cost_estimate=pl.CostEstimate(flops=24 * size * HD, bytes_accessed=2 * size, transcendentals=0),
            name="backward",
        )(*args)
    )
    context = [results.pop(0) for _ in range(blocks)] if first else None
    dq = [results.pop(0) for _ in range(sent)] if last else results.pop(0)
    return context, dq, results if begin > 0 else results[0]


def on_device(halves, seqs, enc_states, norm_gain, kv_weight, queries, cotangent):
    tokens, width = queries.shape
    groups = kv_weight.shape[1] // (2 * HD)
    per_group_heads = width // (groups * HD)
    heads = min(per_group_heads, max(1, 512 // tokens))
    per_group = per_group_heads // heads
    chunks = seqs // max(1, seqs // 2) * groups * per_group
    dims = (chunks, groups, per_group)

    near = max(1, seqs // 2)
    fars = seqs // near

    def from_far(x, shift):
        return lax.ppermute(x, "seq", [(i, (i + shift * near) % seqs) for i in range(seqs)])

    def from_near(x, a, b):
        pairs = []
        for h in range(halves):
            for i in range(seqs):
                to = (h + a) % halves * seqs + i // near * near + (i + b) % near
                pairs.append((h * seqs + i, to))
        return lax.ppermute(x, ("half", "seq"), pairs)

    q_blocks = [queries] + [from_far(queries, s) for s in range(1, fars)]
    own_pairs = project(enc_states, norm_gain, kv_weight)
    order = sorted(
        ((a, b) for a in range(halves) for b in range(near)), key=lambda s: (s[0] > 0 and s[1] > 0, s[1])
    )
    blocks = {(0, 0): [own_pairs]}
    for a, b in order[1:]:
        if a and b:
            across, along = blocks[a, 0][0], blocks[0, b][0]
            middle = across.shape[1] // 2
            upper = from_near(across[:, middle:], 0, b)
            blocks[a, b] = [from_near(along[:, :middle], a, 0), upper]
        else:
            blocks[a, b] = [from_near(own_pairs, a, b)]
    c_own, *_ = lax.optimization_barrier((cotangent, *[blocks[s][0] for s in order[1:3]]))
    c_blocks = [cotangent] + [from_far(c_own, s) for s in range(1, fars)]
    pair_blocks = [blocks[s] for s in order]
    count = len(order)
    q_rows = turn(q_blocks, heads)
    c_rows = turn(c_blocks, heads)

    expos, tops, before = [], [], None
    for i, pairs in enumerate(pair_blocks):
        expo, top, stats, acc = forward(dims, q_rows, c_rows if i == count - 1 else None, pairs, before)
        expos.append(expo)
        tops.append(top)
        before = (stats, acc)
    peers = [from_far(stats, r) for r in range(1, fars)]

    def back(i, span, dq, sums, last):
        return backward(
            dims, q_rows, c_rows, pair_blocks[i], expos[i], tops[i], stats, peers, acc, dq, sums, span, last, tokens
        )

    dq, sends, context_parts = None, [], None
    for i in reversed(range(1, count)):
        parts, dq, dkv = back(i, (0, chunks), dq, None, False)
        if parts is not None:
            context_parts = parts
        sends.append(from_near(dkv, -order[i][0], -order[i][1]))
    split = chunks // fars
    _, away, sums = back(0, (split, chunks), dq, None, True)
    away = [from_far(x, -s) for s, x in enumerate(away, 1)]
    _, (stay,), dkv = back(0, (0, split), dq, sums, True)
    sends.append(dkv)

    def total(arrays):
        return sum(x.astype(f32) for x in arrays).astype(bf16)

    context = total([context_parts[0]] + [from_far(context_parts[s], -s) for s in range(1, fars)])
    d_queries = total([stay, *away])
    d_pairs = total(sends)
    return (context, d_queries, d_pairs)


def solution(mesh):
    shape = mesh.shape
    rows, columns = P(("half", "seq"), None), P(("half", "seq"), "head")

    def body(*args):
        return on_device(shape["half"], shape["seq"], *args)

    return jax.shard_map(
        body,
        mesh=mesh,
        in_specs=(rows, P(), P(None, "head"), columns, columns),
        out_specs=(columns, columns, columns),
        check_vma=False,
    )
```

```python
import functools
import math

import jax
import jax.numpy as jnp
from jax import lax
from jax.experimental import pallas as pl
from jax.experimental.pallas import tpu as pltpu
from jax.sharding import PartitionSpec as P


HD = 64
EPS = 1e-06
LOG2E = math.log2(math.e)
SCALE = HD ** (-0.5)
KEY_ROWS = 256
VMEM_BYTES = 14 << 20
NT = (((1,), (1,)), ((), ()))

bf16 = jnp.bfloat16
f32 = jnp.float32

IN_VMEM = pl.BlockSpec(memory_space=pltpu.VMEM)
IN_PLACE = pl.BlockSpec(memory_space=pl.ANY)


def project_kernel(x_ref, gain_ref, w_ref, out_ref):
    x = x_ref[...].astype(f32)
    inverse_root = lax.rsqrt(jnp.mean(x * x, axis=1, keepdims=True) + EPS)
    normed = (x * inverse_root * gain_ref[...]).astype(bf16)
    pairs = jnp.dot(normed, w_ref[...], preferred_element_type=f32).astype(bf16)
    for g in range(out_ref.shape[0]):
        out_ref[g] = pairs[:, g * 2 * HD : (g + 1) * 2 * HD]


def project(states, gain, weight):
    rows, width = states.shape
    groups = weight.shape[1] // (2 * HD)
    block = min(rows, 512)
    return pl.pallas_call(
        project_kernel,
        grid=(rows // block,),
        in_specs=[
            pl.BlockSpec((block, width), lambda i: (i, 0)),
            pl.BlockSpec((1, width), lambda i: (0, 0)),
            pl.BlockSpec((width, weight.shape[1]), lambda i: (0, 0)),
        ],
        out_specs=pl.BlockSpec((groups, block, 2 * HD), lambda i: (0, i, 0)),
        out_shape=jax.ShapeDtypeStruct((groups, rows, 2 * HD), bf16),
        compiler_params=pltpu.CompilerParams(vmem_limit_bytes=57 << 20),
        cost_estimate=pl.CostEstimate(
            flops=2 * rows * width * weight.shape[1], bytes_accessed=2 * rows * width, transcendentals=0
        ),
        name="project",
    )(states, gain.reshape(1, width), weight)


def turn_kernel(count, *refs):
    inputs, out_ref = refs[:count], refs[count]
    chunks, _, lanes = out_ref.shape
    per_block = chunks // count
    tokens = inputs[0].shape[0]
    heads = lanes // tokens
    for s in range(count):
        turned = inputs[s][...].T
        for i in range(per_block):
            base = i * heads * HD
            out_ref[s * per_block + i] = jnp.concatenate(
                [turned[base + h * HD : base + (h + 1) * HD] for h in range(heads)], axis=1
            )


def turn(blocks, heads):
    tokens, width = blocks[0].shape
    chunks = len(blocks) * width // (heads * HD)
    return pl.pallas_call(
        functools.partial(turn_kernel, len(blocks)),
        in_specs=[IN_VMEM] * len(blocks),
        out_specs=IN_VMEM,
        out_shape=jax.ShapeDtypeStruct((chunks, HD, heads * tokens), bf16),
        compiler_params=pltpu.CompilerParams(vmem_limit_bytes=VMEM_BYTES),
        name="turn",
    )(*blocks)


def gathered(piece_refs, whole_ref):
    if len(piece_refs) == 1:
        return piece_refs[0]
    begin = 0
    for piece in piece_refs:
        rows = piece.shape[1]
        whole_ref[:, begin : begin + rows] = piece[...]
        begin += rows
    return whole_ref


def forward_kernel(dims, pieces, first, last, *refs):
    chunks, groups, per_group = dims
    refs = list(refs)
    q_ref = refs.pop(0)
    c_ref = refs.pop(0) if last else None
    piece_refs = [refs.pop(0) for _ in range(pieces)]
    past, past_acc = (None, None) if first else (refs.pop(0), refs.pop(0))
    e_ref, top_ref, st_ref, acc_ref, whole_ref, value_t, scores, expo = refs
    kv_ref = gathered(piece_refs, whole_ref)
    length = kv_ref.shape[1]
    lanes = q_ref.shape[2]
    pad = jnp.zeros((HD, lanes), bf16)
    steps = length // KEY_ROWS
    for g in range(groups):
        value_t[g, :HD] = kv_ref[g].T[HD:]
        value_t[g, HD:] = jnp.ones((16, length), bf16)

    def group_of(c):
        return (c // per_group) % groups

    def emit(ca, cb, cc, slot, top):
        largest, total = None, None
        if ca is not None:
            weights = jnp.concatenate([q_ref[ca] * jnp.asarray(SCALE, bf16), pad], axis=0)
            ga = group_of(ca)
        if cb is not None:
            low_top = top * LOG2E
        if cc is not None:
            gc = group_of(cc)
        for k in range(steps):
            ks = slice(k * KEY_ROWS, (k + 1) * KEY_ROWS)
            if cb is not None:
                weight = jnp.exp2(scores[ks] * LOG2E - low_top).astype(bf16)
                expo[slot, ks] = weight
                e_ref[cb, ks] = weight
            if ca is not None:
                s = jnp.dot(kv_ref[ga, ks], weights, preferred_element_type=f32)
                scores[ks] = s
                part = jnp.max(s.reshape(KEY_ROWS // 8, 8, lanes), axis=0)
                largest = part if largest is None else jnp.maximum(largest, part)
            if cc is not None:
                part = jnp.dot(value_t[gc, :, ks], expo[1 - slot, ks], preferred_element_type=f32)
                total = part if total is None else total + part
        if cb is not None:
            top_ref[pl.ds(cb, 1)] = top
        if cc is not None:
            m = top_ref[pl.ds(cc, 1)]
            l = total[HD : HD + 1]
            acc = total[:HD]
            if not first:
                before = past[0, pl.ds(cc, 1)]
                both = jnp.maximum(before, m)
                old, new = jnp.exp(before - both), jnp.exp(m - both)
                l = past[1, pl.ds(cc, 1)] * old + l * new
                acc = past_acc[cc] * old + acc * new
                m = both
            st_ref[0, pl.ds(cc, 1)] = m
            st_ref[1, pl.ds(cc, 1)] = l
            if last:
                st_ref[2, pl.ds(cc, 1)] = jnp.sum(c_ref[cc].astype(f32) * acc, axis=0, keepdims=True)
            acc_ref[cc] = acc
        return None if largest is None else jnp.max(largest, axis=0, keepdims=True)

    n = chunks
    top = emit(0, None, None, None, None)
    top = emit(1, 0, None, 0, top)

    def body(j, top):
        top = emit(2 * j + 2, 2 * j + 1, 2 * j, 1, top)
        return emit(2 * j + 3, 2 * j + 2, 2 * j + 1, 0, top)

    top = lax.fori_loop(0, n // 2 - 1, body, top)
    emit(None, n - 1, n - 2, 1, top)
    emit(None, None, n - 1, 0, None)


def forward(dims, q_rows, c_rows, pairs, before):
    chunks, groups, _ = dims
    lanes = q_rows.shape[2]
    length = sum(p.shape[1] for p in pairs)
    first, last = before is None, c_rows is not None
    args = [q_rows] + ([c_rows] if last else []) + pairs + ([] if first else list(before))
    size = chunks * lanes * length
    return pl.pallas_call(
        functools.partial(forward_kernel, dims, len(pairs), first, last),
        in_specs=[IN_VMEM] * len(args),
        out_specs=[IN_VMEM] * 4,
        out_shape=[
            jax.ShapeDtypeStruct((chunks, length, lanes), bf16),
            jax.ShapeDtypeStruct((chunks, lanes), f32),
            jax.ShapeDtypeStruct((3 if last else 2, chunks, lanes), f32),
            jax.ShapeDtypeStruct((chunks, HD, lanes), f32),
        ],
        scratch_shapes=[
            pltpu.VMEM((groups, length, 2 * HD), bf16),
            pltpu.VMEM((groups, HD + 16, length), bf16),
            pltpu.VMEM((length, lanes), f32),
            pltpu.VMEM((2, length, lanes), bf16),
        ],
        compiler_params=pltpu.CompilerParams(vmem_limit_bytes=VMEM_BYTES),
        cost_estimate=pl.CostEstimate(flops=16 * size * HD, bytes_accessed=2 * size, transcendentals=size),
        name="forward",
    )(*args)


def rolled(rows, shift):
    count = rows.shape[0]
    shift = shift % count
    return rows if shift == 0 else jnp.concatenate([rows[count - shift :], rows[: count - shift]], axis=0)


def backward_kernel(dims, pieces, peers, span, first, last, *refs):
    chunks, groups, per_group = dims
    begin, end = span
    blocks = peers + 1
    per_block = chunks // blocks
    whole_span = span == (0, chunks)
    refs = list(refs)
    q_ref, c_ref = refs.pop(0), refs.pop(0)
    piece_refs = [refs.pop(0) for _ in range(pieces)]
    e_ref, top_ref, own_ref = [refs.pop(0) for _ in range(3)]
    peer_refs = [refs.pop(0) for _ in range(peers)]
    acc_ref = refs.pop(0) if first else None
    past_dq = None if first else refs.pop(0)
    past_sums = [refs.pop(0), refs.pop(0)] if begin == 0 and not whole_span else None
    ctx_outs = [refs.pop(0) for _ in range(blocks)] if first else None
    sent = list(range(begin // per_block, end // per_block))
    dq_outs = [refs.pop(0) for _ in sent] if last else [refs.pop(0)]
    outs = [refs.pop(0)] if begin == 0 else [refs.pop(0), refs.pop(0)]
    whole_ref, key_t, score_grad, key_sum, value_sum, factor, delta, rows, row_sem = refs
    kv_ref = gathered(piece_refs, whole_ref)
    length = kv_ref.shape[1]
    lanes = q_ref.shape[2]
    steps = length // KEY_ROWS
    tokens = rows.shape[1]
    heads = lanes // tokens
    pad = jnp.zeros((HD, lanes), bf16)

    def group_of(c):
        return (c // per_group) % groups

    for g in range(groups):
        key_t[g] = kv_ref[g].T[:HD]
    key_sum[...] = jnp.zeros_like(key_sum) if past_sums is None else past_sums[0][...]
    value_sum[...] = jnp.zeros_like(value_sum) if past_sums is None else past_sums[1][...]

    stats = [[own_ref[i] for i in range(3)]]
    for r in range(1, blocks):
        stats.append([rolled(peer_refs[r - 1][i], r * per_block) for i in range(3)])
    top = functools.reduce(jnp.maximum, [s[0] for s in stats])
    shares = [jnp.exp(s[0] - top) for s in stats]
    total = sum(s[1] * w for s, w in zip(stats, shares))
    delta[...] = sum(s[2] * w for s, w in zip(stats, shares)) / total
    factor[0] = jnp.exp(top_ref[...] - top) / total
    if first:
        factor[1] = shares[0] / total

    def put_rows(c, value):
        flat = jnp.concatenate([value[:, h * tokens : (h + 1) * tokens] for h in range(heads)], axis=0)
        offset = pl.multiple_of((c % per_block) * heads * HD, heads * HD)
        rows[c // per_block, :, pl.ds(offset, heads * HD)] = flat.astype(bf16).T

    def send_rows(which, refs):
        copies = [pltpu.make_async_copy(rows.at[s], ref, row_sem.at[s]) for s, ref in zip(which, refs)]
        for copy in copies:
            copy.start()
        for copy in copies:
            copy.wait()

    if first:

        def put_context(c, _):
            put_rows(c, acc_ref[c] * factor[1, pl.ds(c, 1)])
            return 0

        lax.fori_loop(0, chunks, put_context, 0)
        send_rows(range(blocks), ctx_outs)

    def emit(ca, cb):
        if ca is not None:
            ga = group_of(ca)
            weights = jnp.concatenate([pad, c_ref[ca]], axis=0)
            fa, da = factor[0, pl.ds(ca, 1)], delta[pl.ds(ca, 1)]
            scaled_c = (c_ref[ca].astype(f32) * fa).astype(bf16)
        if cb is not None:
            gb = group_of(cb)
            fb = factor[0, pl.ds(cb, 1)] * SCALE
            scaled_q = (q_ref[cb].astype(f32) * fb).astype(bf16)
            dq = None
        for k in range(steps):
            ks = slice(k * KEY_ROWS, (k + 1) * KEY_ROWS)
            if cb is not None:
                ds = score_grad[ks]
                part = jnp.dot(key_t[gb, :, ks], ds, preferred_element_type=f32)
                dq = part if dq is None else dq + part
                key_sum[gb, :, ks] += lax.dot_general(scaled_q, ds, NT, preferred_element_type=f32)
            if ca is not None:
                e = e_ref[ca, ks]
                prob_grad = jnp.dot(kv_ref[ga, ks], weights, preferred_element_type=f32)
                score_grad[ks] = (e.astype(f32) * (prob_grad - da)).astype(bf16)
                value_sum[ga, :, ks] += lax.dot_general(scaled_c, e, NT, preferred_element_type=f32)
        if cb is not None:
            dq = dq * fb
            if not first:
                dq = dq + past_dq[cb]
            if last:
                put_rows(cb, dq)
            else:
                dq_outs[0][cb] = dq

    emit(begin, None)

    def body(j, _):
        c = begin + 2 * j
        emit(c + 1, c)
        emit(c + 2, c + 1)
        return 0

    lax.fori_loop(0, (end - begin) // 2 - 1, body, 0)
    emit(end - 1, end - 2)
    emit(None, end - 1)
    if last:
        send_rows(sent, dq_outs)
    if begin > 0:
        outs[0][...] = key_sum[...]
        outs[1][...] = value_sum[...]
    else:
        for g in range(groups):
            both = jnp.concatenate([key_sum[g].astype(bf16), value_sum[g].astype(bf16)], axis=0)
            outs[0][:, g * 2 * HD : (g + 1) * 2 * HD] = both.T


def backward(dims, q_rows, c_rows, pairs, expo, top, own, peers, acc, past_dq, past_sums, span, last, tokens):
    chunks, groups, _ = dims
    begin, end = span
    lanes = q_rows.shape[2]
    length = sum(p.shape[1] for p in pairs)
    first = past_dq is None
    blocks = len(peers) + 1
    per_block = chunks // blocks
    width = per_block * (lanes // tokens) * HD
    args = [q_rows, c_rows, *pairs, expo, top, own, *peers] + [acc if first else past_dq] + list(past_sums or [])
    row_block = jax.ShapeDtypeStruct((tokens, width), bf16)
    sums = jax.ShapeDtypeStruct((groups, HD, length), f32)
    outs, out_specs = [], []
    if first:
        outs += [row_block] * blocks
        out_specs += [IN_PLACE] * blocks
    sent = (end - begin) // per_block
    if last:
        outs += [row_block] * sent
        out_specs += [IN_PLACE] * sent
    else:
        outs.append(jax.ShapeDtypeStruct((chunks, HD, lanes), f32))
        out_specs.append(IN_VMEM)
    if begin > 0:
        outs += [sums] * 2
        out_specs += [IN_VMEM] * 2
    else:
        outs.append(jax.ShapeDtypeStruct((length, groups * 2 * HD), bf16))
        out_specs.append(IN_VMEM)
    size = (end - begin) * lanes * length
    results = list(
        pl.pallas_call(
            functools.partial(backward_kernel, dims, len(pairs), len(peers), span, first, last),
            in_specs=[IN_VMEM] * len(args),
            out_specs=out_specs,
            out_shape=outs,
            scratch_shapes=[
                pltpu.VMEM((groups, length, 2 * HD), bf16),
                pltpu.VMEM((groups, HD, length), bf16),
                pltpu.VMEM((length, lanes), bf16),
                pltpu.VMEM((groups, HD, length), f32),
                pltpu.VMEM((groups, HD, length), f32),
                pltpu.VMEM((2, chunks, lanes), f32),
                pltpu.VMEM((chunks, lanes), f32),
                pltpu.VMEM((blocks, tokens, width), bf16),
                pltpu.SemaphoreType.DMA((blocks,)),
            ],
            compiler_params=pltpu.CompilerParams(vmem_limit_bytes=VMEM_BYTES),
            cost_estimate=pl.CostEstimate(flops=24 * size * HD, bytes_accessed=2 * size, transcendentals=0),
            name="backward",
        )(*args)
    )
    context = [results.pop(0) for _ in range(blocks)] if first else None
    dq = [results.pop(0) for _ in range(sent)] if last else results.pop(0)
    return context, dq, results if begin > 0 else results[0]


def on_device(halves, seqs, enc_states, norm_gain, kv_weight, queries, cotangent):
    tokens, width = queries.shape
    groups = kv_weight.shape[1] // (2 * HD)
    per_group_heads = width // (groups * HD)
    heads = min(per_group_heads, max(1, 512 // tokens))
    per_group = per_group_heads // heads
    chunks = seqs // max(1, seqs // 2) * groups * per_group
    dims = (chunks, groups, per_group)

    near = max(1, seqs // 2)
    fars = seqs // near

    def from_far(x, shift):
        return lax.ppermute(x, "seq", [(i, (i + shift * near) % seqs) for i in range(seqs)])

    def from_near(x, a, b):
        pairs = []
        for h in range(halves):
            for i in range(seqs):
                to = (h + a) % halves * seqs + i // near * near + (i + b) % near
                pairs.append((h * seqs + i, to))
        return lax.ppermute(x, ("half", "seq"), pairs)

    q_blocks = [queries] + [from_far(queries, s) for s in range(1, fars)]
    own_pairs = project(enc_states, norm_gain, kv_weight)
    order = sorted(
        ((a, b) for a in range(halves) for b in range(near)), key=lambda s: (s[0] > 0 and s[1] > 0, s[1])
    )
    blocks = {(0, 0): [own_pairs]}
    for a, b in order[1:]:
        if a and b:
            across, along = blocks[a, 0][0], blocks[0, b][0]
            middle = across.shape[1] // 2
            upper = from_near(across[:, middle:], 0, b)
            blocks[a, b] = [from_near(along[:, :middle], a, 0), upper]
        else:
            blocks[a, b] = [from_near(own_pairs, a, b)]
    c_own, *_ = lax.optimization_barrier((cotangent, *[blocks[s][0] for s in order[1:2]]))
    c_blocks = [cotangent] + [from_far(c_own, s) for s in range(1, fars)]
    pair_blocks = [blocks[s] for s in order]
    count = len(order)
    q_rows = turn(q_blocks, heads)
    c_rows = turn(c_blocks, heads)

    expos, tops, before = [], [], None
    for i, pairs in enumerate(pair_blocks):
        expo, top, stats, acc = forward(dims, q_rows, c_rows if i == count - 1 else None, pairs, before)
        expos.append(expo)
        tops.append(top)
        before = (stats, acc)
    peers = [from_far(stats, r) for r in range(1, fars)]

    def back(i, span, dq, sums, last):
        return backward(
            dims, q_rows, c_rows, pair_blocks[i], expos[i], tops[i], stats, peers, acc, dq, sums, span, last, tokens
        )

    dq, sends, context_parts = None, [], None
    for i in reversed(range(1, count)):
        parts, dq, dkv = back(i, (0, chunks), dq, None, False)
        if parts is not None:
            context_parts = parts
        sends.append(from_near(dkv, -order[i][0], -order[i][1]))
    split = chunks // fars
    _, away, sums = back(0, (split, chunks), dq, None, True)
    away = [from_far(x, -s) for s, x in enumerate(away, 1)]
    _, (stay,), dkv = back(0, (0, split), dq, sums, True)
    sends.append(dkv)

    def total(arrays):
        return sum(x.astype(f32) for x in arrays).astype(bf16)

    context = total([context_parts[0]] + [from_far(context_parts[s], -s) for s in range(1, fars)])
    d_pairs = total(sends)
    d_queries = total([stay, *away])
    return (context, d_queries, d_pairs)


def solution(mesh):
    shape = mesh.shape
    rows, columns = P(("half", "seq"), None), P(("half", "seq"), "head")

    def body(*args):
        return on_device(shape["half"], shape["seq"], *args)

    return jax.shard_map(
        body,
        mesh=mesh,
        in_specs=(rows, P(), P(None, "head"), columns, columns),
        out_specs=(columns, columns, columns),
        check_vma=False,
    )
```

```python
import functools
import math

import jax
import jax.numpy as jnp
from jax import lax
from jax.experimental import pallas as pl
from jax.experimental.pallas import tpu as pltpu
from jax.sharding import PartitionSpec as P


HD = 64
EPS = 1e-06
LOG2E = math.log2(math.e)
SCALE = HD ** (-0.5)
KEY_ROWS = 256
GRAD_ROWS = 256
VMEM_BYTES = 14 << 20
NT = (((1,), (1,)), ((), ()))

bf16 = jnp.bfloat16
f32 = jnp.float32

IN_VMEM = pl.BlockSpec(memory_space=pltpu.VMEM)
IN_PLACE = pl.BlockSpec(memory_space=pl.ANY)


def project_kernel(x_ref, gain_ref, w_ref, out_ref):
    x = x_ref[...].astype(f32)
    inverse_root = lax.rsqrt(jnp.mean(x * x, axis=1, keepdims=True) + EPS)
    normed = (x * inverse_root * gain_ref[...]).astype(bf16)
    pairs = jnp.dot(normed, w_ref[...], preferred_element_type=f32).astype(bf16)
    for g in range(out_ref.shape[0]):
        out_ref[g] = pairs[:, g * 2 * HD : (g + 1) * 2 * HD]


def project(states, gain, weight):
    rows, width = states.shape
    groups = weight.shape[1] // (2 * HD)
    block = min(rows, 512)
    return pl.pallas_call(
        project_kernel,
        grid=(rows // block,),
        in_specs=[
            pl.BlockSpec((block, width), lambda i: (i, 0)),
            pl.BlockSpec((1, width), lambda i: (0, 0)),
            pl.BlockSpec((width, weight.shape[1]), lambda i: (0, 0)),
        ],
        out_specs=pl.BlockSpec((groups, block, 2 * HD), lambda i: (0, i, 0)),
        out_shape=jax.ShapeDtypeStruct((groups, rows, 2 * HD), bf16),
        compiler_params=pltpu.CompilerParams(vmem_limit_bytes=57 << 20),
        cost_estimate=pl.CostEstimate(
            flops=2 * rows * width * weight.shape[1], bytes_accessed=2 * rows * width, transcendentals=0
        ),
        name="project",
    )(states, gain.reshape(1, width), weight)


def turn_kernel(count, *refs):
    inputs, out_ref = refs[:count], refs[count]
    chunks, _, lanes = out_ref.shape
    per_block = chunks // count
    tokens = inputs[0].shape[0]
    heads = lanes // tokens
    for s in range(count):
        turned = inputs[s][...].T
        for i in range(per_block):
            base = i * heads * HD
            out_ref[s * per_block + i] = jnp.concatenate(
                [turned[base + h * HD : base + (h + 1) * HD] for h in range(heads)], axis=1
            )


def turn(blocks, heads):
    tokens, width = blocks[0].shape
    chunks = len(blocks) * width // (heads * HD)
    return pl.pallas_call(
        functools.partial(turn_kernel, len(blocks)),
        in_specs=[IN_VMEM] * len(blocks),
        out_specs=IN_VMEM,
        out_shape=jax.ShapeDtypeStruct((chunks, HD, heads * tokens), bf16),
        compiler_params=pltpu.CompilerParams(vmem_limit_bytes=VMEM_BYTES),
        name="turn",
    )(*blocks)


def gathered(piece_refs, whole_ref):
    if len(piece_refs) == 1:
        return piece_refs[0]
    begin = 0
    for piece in piece_refs:
        rows = piece.shape[1]
        whole_ref[:, begin : begin + rows] = piece[...]
        begin += rows
    return whole_ref


def forward_kernel(dims, pieces, first, last, *refs):
    chunks, groups, per_group = dims
    refs = list(refs)
    q_ref = refs.pop(0)
    c_ref = refs.pop(0) if last else None
    piece_refs = [refs.pop(0) for _ in range(pieces)]
    past, past_acc = (None, None) if first else (refs.pop(0), refs.pop(0))
    e_ref, top_ref, st_ref, acc_ref, whole_ref, value_t, scores, expo = refs
    kv_ref = gathered(piece_refs, whole_ref)
    length = kv_ref.shape[1]
    lanes = q_ref.shape[2]
    pad = jnp.zeros((HD, lanes), bf16)
    steps = length // KEY_ROWS
    for g in range(groups):
        value_t[g, :HD] = kv_ref[g].T[HD:]
        value_t[g, HD:] = jnp.ones((16, length), bf16)

    def group_of(c):
        return (c // per_group) % groups

    def emit(ca, cb, cc, slot, top):
        largest, total = None, None
        if ca is not None:
            weights = jnp.concatenate([q_ref[ca] * jnp.asarray(SCALE, bf16), pad], axis=0)
            ga = group_of(ca)
        if cb is not None:
            low_top = top * LOG2E
        if cc is not None:
            gc = group_of(cc)
        for k in range(steps):
            ks = slice(k * KEY_ROWS, (k + 1) * KEY_ROWS)
            if cb is not None:
                weight = jnp.exp2(scores[ks] * LOG2E - low_top).astype(bf16)
                expo[slot, ks] = weight
                e_ref[cb, ks] = weight
            if ca is not None:
                s = jnp.dot(kv_ref[ga, ks], weights, preferred_element_type=f32)
                scores[ks] = s
                part = jnp.max(s.reshape(KEY_ROWS // 8, 8, lanes), axis=0)
                largest = part if largest is None else jnp.maximum(largest, part)
            if cc is not None:
                part = jnp.dot(value_t[gc, :, ks], expo[1 - slot, ks], preferred_element_type=f32)
                total = part if total is None else total + part
        if cb is not None:
            top_ref[pl.ds(cb, 1)] = top
        if cc is not None:
            m = top_ref[pl.ds(cc, 1)]
            l = total[HD : HD + 1]
            acc = total[:HD]
            if not first:
                before = past[0, pl.ds(cc, 1)]
                both = jnp.maximum(before, m)
                old, new = jnp.exp(before - both), jnp.exp(m - both)
                l = past[1, pl.ds(cc, 1)] * old + l * new
                acc = past_acc[cc] * old + acc * new
                m = both
            st_ref[0, pl.ds(cc, 1)] = m
            st_ref[1, pl.ds(cc, 1)] = l
            if last:
                st_ref[2, pl.ds(cc, 1)] = jnp.sum(c_ref[cc].astype(f32) * acc, axis=0, keepdims=True)
            acc_ref[cc] = acc
        return None if largest is None else jnp.max(largest, axis=0, keepdims=True)

    n = chunks
    top = emit(0, None, None, None, None)
    top = emit(1, 0, None, 0, top)

    def body(j, top):
        top = emit(2 * j + 2, 2 * j + 1, 2 * j, 1, top)
        return emit(2 * j + 3, 2 * j + 2, 2 * j + 1, 0, top)

    top = lax.fori_loop(0, n // 2 - 1, body, top)
    emit(None, n - 1, n - 2, 1, top)
    emit(None, None, n - 1, 0, None)


def forward(dims, q_rows, c_rows, pairs, before):
    chunks, groups, _ = dims
    lanes = q_rows.shape[2]
    length = sum(p.shape[1] for p in pairs)
    first, last = before is None, c_rows is not None
    args = [q_rows] + ([c_rows] if last else []) + pairs + ([] if first else list(before))
    size = chunks * lanes * length
    return pl.pallas_call(
        functools.partial(forward_kernel, dims, len(pairs), first, last),
        in_specs=[IN_VMEM] * len(args),
        out_specs=[IN_VMEM] * 4,
        out_shape=[
            jax.ShapeDtypeStruct((chunks, length, lanes), bf16),
            jax.ShapeDtypeStruct((chunks, lanes), f32),
            jax.ShapeDtypeStruct((3 if last else 2, chunks, lanes), f32),
            jax.ShapeDtypeStruct((chunks, HD, lanes), f32),
        ],
        scratch_shapes=[
            pltpu.VMEM((groups, length, 2 * HD), bf16),
            pltpu.VMEM((groups, HD + 16, length), bf16),
            pltpu.VMEM((length, lanes), f32),
            pltpu.VMEM((2, length, lanes), bf16),
        ],
        compiler_params=pltpu.CompilerParams(vmem_limit_bytes=VMEM_BYTES),
        cost_estimate=pl.CostEstimate(flops=16 * size * HD, bytes_accessed=2 * size, transcendentals=size),
        name="forward",
    )(*args)


def rolled(rows, shift):
    count = rows.shape[0]
    shift = shift % count
    return rows if shift == 0 else jnp.concatenate([rows[count - shift :], rows[: count - shift]], axis=0)


def backward_kernel(dims, pieces, peers, span, first, last, *refs):
    chunks, groups, per_group = dims
    begin, end = span
    blocks = peers + 1
    per_block = chunks // blocks
    whole_span = span == (0, chunks)
    refs = list(refs)
    q_ref, c_ref = refs.pop(0), refs.pop(0)
    piece_refs = [refs.pop(0) for _ in range(pieces)]
    e_ref, top_ref, own_ref = [refs.pop(0) for _ in range(3)]
    peer_refs = [refs.pop(0) for _ in range(peers)]
    acc_ref = refs.pop(0) if first else None
    past_dq = None if first else refs.pop(0)
    past_sums = [refs.pop(0), refs.pop(0)] if begin == 0 and not whole_span else None
    ctx_outs = [refs.pop(0) for _ in range(blocks)] if first else None
    sent = list(range(begin // per_block, end // per_block))
    dq_outs = [refs.pop(0) for _ in sent] if last else [refs.pop(0)]
    outs = [refs.pop(0)] if begin == 0 else [refs.pop(0), refs.pop(0)]
    whole_ref, key_t, score_grad, key_sum, value_sum, factor, delta, rows, row_sem = refs
    kv_ref = gathered(piece_refs, whole_ref)
    length = kv_ref.shape[1]
    lanes = q_ref.shape[2]
    steps = length // GRAD_ROWS
    tokens = rows.shape[1]
    heads = lanes // tokens
    pad = jnp.zeros((HD, lanes), bf16)

    def group_of(c):
        return (c // per_group) % groups

    for g in range(groups):
        key_t[g] = kv_ref[g].T[:HD]
    key_sum[...] = jnp.zeros_like(key_sum) if past_sums is None else past_sums[0][...]
    value_sum[...] = jnp.zeros_like(value_sum) if past_sums is None else past_sums[1][...]

    stats = [[own_ref[i] for i in range(3)]]
    for r in range(1, blocks):
        stats.append([rolled(peer_refs[r - 1][i], r * per_block) for i in range(3)])
    top = functools.reduce(jnp.maximum, [s[0] for s in stats])
    shares = [jnp.exp(s[0] - top) for s in stats]
    total = sum(s[1] * w for s, w in zip(stats, shares))
    delta[...] = sum(s[2] * w for s, w in zip(stats, shares)) / total
    factor[0] = jnp.exp(top_ref[...] - top) / total
    if first:
        factor[1] = shares[0] / total

    def put_rows(c, value):
        flat = jnp.concatenate([value[:, h * tokens : (h + 1) * tokens] for h in range(heads)], axis=0)
        offset = pl.multiple_of((c % per_block) * heads * HD, heads * HD)
        rows[c // per_block, :, pl.ds(offset, heads * HD)] = flat.astype(bf16).T

    def send_rows(which, refs):
        copies = [pltpu.make_async_copy(rows.at[s], ref, row_sem.at[s]) for s, ref in zip(which, refs)]
        for copy in copies:
            copy.start()
        for copy in copies:
            copy.wait()

    if first:

        def put_context(c, _):
            put_rows(c, acc_ref[c] * factor[1, pl.ds(c, 1)])
            return 0

        lax.fori_loop(0, chunks, put_context, 0)
        send_rows(range(blocks), ctx_outs)

    def emit(ca, cb):
        if ca is not None:
            ga = group_of(ca)
            weights = jnp.concatenate([pad, c_ref[ca]], axis=0)
            fa, da = factor[0, pl.ds(ca, 1)], delta[pl.ds(ca, 1)]
            scaled_c = (c_ref[ca].astype(f32) * fa).astype(bf16)
        if cb is not None:
            gb = group_of(cb)
            fb = factor[0, pl.ds(cb, 1)] * SCALE
            scaled_q = (q_ref[cb].astype(f32) * fb).astype(bf16)
            dq = None
        for k in range(steps):
            ks = slice(k * GRAD_ROWS, (k + 1) * GRAD_ROWS)
            if cb is not None:
                ds = score_grad[ks]
                part = jnp.dot(key_t[gb, :, ks], ds, preferred_element_type=f32)
                dq = part if dq is None else dq + part
                key_sum[gb, :, ks] += lax.dot_general(scaled_q, ds, NT, preferred_element_type=f32)
            if ca is not None:
                e = e_ref[ca, ks]
                prob_grad = jnp.dot(kv_ref[ga, ks], weights, preferred_element_type=f32)
                score_grad[ks] = (e.astype(f32) * (prob_grad - da)).astype(bf16)
                value_sum[ga, :, ks] += lax.dot_general(scaled_c, e, NT, preferred_element_type=f32)
        if cb is not None:
            dq = dq * fb
            if not first:
                dq = dq + past_dq[cb]
            if last:
                put_rows(cb, dq)
            else:
                dq_outs[0][cb] = dq

    emit(begin, None)

    def body(j, _):
        c = begin + 2 * j
        emit(c + 1, c)
        emit(c + 2, c + 1)
        return 0

    lax.fori_loop(0, (end - begin) // 2 - 1, body, 0)
    emit(end - 1, end - 2)
    emit(None, end - 1)
    if last:
        send_rows(sent, dq_outs)
    if begin > 0:
        outs[0][...] = key_sum[...]
        outs[1][...] = value_sum[...]
    else:
        for g in range(groups):
            both = jnp.concatenate([key_sum[g].astype(bf16), value_sum[g].astype(bf16)], axis=0)
            outs[0][:, g * 2 * HD : (g + 1) * 2 * HD] = both.T


def backward(dims, q_rows, c_rows, pairs, expo, top, own, peers, acc, past_dq, past_sums, span, last, tokens):
    chunks, groups, _ = dims
    begin, end = span
    lanes = q_rows.shape[2]
    length = sum(p.shape[1] for p in pairs)
    first = past_dq is None
    blocks = len(peers) + 1
    per_block = chunks // blocks
    width = per_block * (lanes // tokens) * HD
    args = [q_rows, c_rows, *pairs, expo, top, own, *peers] + [acc if first else past_dq] + list(past_sums or [])
    row_block = jax.ShapeDtypeStruct((tokens, width), bf16)
    sums = jax.ShapeDtypeStruct((groups, HD, length), f32)
    outs, out_specs = [], []
    if first:
        outs += [row_block] * blocks
        out_specs += [IN_PLACE] * blocks
    sent = (end - begin) // per_block
    if last:
        outs += [row_block] * sent
        out_specs += [IN_PLACE] * sent
    else:
        outs.append(jax.ShapeDtypeStruct((chunks, HD, lanes), f32))
        out_specs.append(IN_VMEM)
    if begin > 0:
        outs += [sums] * 2
        out_specs += [IN_VMEM] * 2
    else:
        outs.append(jax.ShapeDtypeStruct((length, groups * 2 * HD), bf16))
        out_specs.append(IN_VMEM)
    size = (end - begin) * lanes * length
    results = list(
        pl.pallas_call(
            functools.partial(backward_kernel, dims, len(pairs), len(peers), span, first, last),
            in_specs=[IN_VMEM] * len(args),
            out_specs=out_specs,
            out_shape=outs,
            scratch_shapes=[
                pltpu.VMEM((groups, length, 2 * HD), bf16),
                pltpu.VMEM((groups, HD, length), bf16),
                pltpu.VMEM((length, lanes), bf16),
                pltpu.VMEM((groups, HD, length), f32),
                pltpu.VMEM((groups, HD, length), f32),
                pltpu.VMEM((2, chunks, lanes), f32),
                pltpu.VMEM((chunks, lanes), f32),
                pltpu.VMEM((blocks, tokens, width), bf16),
                pltpu.SemaphoreType.DMA((blocks,)),
            ],
            compiler_params=pltpu.CompilerParams(vmem_limit_bytes=VMEM_BYTES),
            cost_estimate=pl.CostEstimate(flops=24 * size * HD, bytes_accessed=2 * size, transcendentals=0),
            name="backward",
        )(*args)
    )
    context = [results.pop(0) for _ in range(blocks)] if first else None
    dq = [results.pop(0) for _ in range(sent)] if last else results.pop(0)
    return context, dq, results if begin > 0 else results[0]


def on_device(halves, seqs, enc_states, norm_gain, kv_weight, queries, cotangent):
    tokens, width = queries.shape
    groups = kv_weight.shape[1] // (2 * HD)
    per_group_heads = width // (groups * HD)
    heads = min(per_group_heads, max(1, 512 // tokens))
    per_group = per_group_heads // heads
    chunks = seqs // max(1, seqs // 2) * groups * per_group
    dims = (chunks, groups, per_group)

    near = max(1, seqs // 2)
    fars = seqs // near

    def from_far(x, shift):
        return lax.ppermute(x, "seq", [(i, (i + shift * near) % seqs) for i in range(seqs)])

    def from_near(x, a, b):
        pairs = []
        for h in range(halves):
            for i in range(seqs):
                to = (h + a) % halves * seqs + i // near * near + (i + b) % near
                pairs.append((h * seqs + i, to))
        return lax.ppermute(x, ("half", "seq"), pairs)

    q_blocks = [queries] + [from_far(queries, s) for s in range(1, fars)]
    own_pairs = project(enc_states, norm_gain, kv_weight)
    order = sorted(
        ((a, b) for a in range(halves) for b in range(near)), key=lambda s: (s[0] > 0 and s[1] > 0, s[1])
    )
    blocks = {(0, 0): [own_pairs]}
    for a, b in order[1:]:
        if a and b:
            across, along = blocks[a, 0][0], blocks[0, b][0]
            middle = across.shape[1] // 2
            upper = from_near(across[:, middle:], 0, b)
            blocks[a, b] = [from_near(along[:, :middle], a, 0), upper]
        else:
            blocks[a, b] = [from_near(own_pairs, a, b)]
    c_own, *_ = lax.optimization_barrier((cotangent, *[blocks[s][0] for s in order[1:2]]))
    c_blocks = [cotangent] + [from_far(c_own, s) for s in range(1, fars)]
    pair_blocks = [blocks[s] for s in order]
    count = len(order)
    q_rows = turn(q_blocks, heads)
    c_rows = turn(c_blocks, heads)

    expos, tops, before = [], [], None
    for i, pairs in enumerate(pair_blocks):
        expo, top, stats, acc = forward(dims, q_rows, c_rows if i == count - 1 else None, pairs, before)
        expos.append(expo)
        tops.append(top)
        before = (stats, acc)
    peers = [from_far(stats, r) for r in range(1, fars)]

    def back(i, span, dq, sums, last):
        return backward(
            dims, q_rows, c_rows, pair_blocks[i], expos[i], tops[i], stats, peers, acc, dq, sums, span, last, tokens
        )

    dq, sends, context_parts = None, [], None
    for i in reversed(range(1, count)):
        parts, dq, dkv = back(i, (0, chunks), dq, None, False)
        if parts is not None:
            context_parts = parts
        sends.append(from_near(dkv, -order[i][0], -order[i][1]))
    split = chunks // fars
    _, away, sums = back(0, (split, chunks), dq, None, True)
    away = [from_far(x, -s) for s, x in enumerate(away, 1)]
    _, (stay,), dkv = back(0, (0, split), dq, sums, True)
    sends.append(dkv)

    def total(arrays):
        return sum(x.astype(f32) for x in arrays).astype(bf16)

    context = total([context_parts[0]] + [from_far(context_parts[s], -s) for s in range(1, fars)])
    d_pairs = total(sends)
    d_queries = total([stay, *away])
    return (context, d_queries, d_pairs)


def solution(mesh):
    shape = mesh.shape
    rows, columns = P(("half", "seq"), None), P(("half", "seq"), "head")

    def body(*args):
        return on_device(shape["half"], shape["seq"], *args)

    return jax.shard_map(
        body,
        mesh=mesh,
        in_specs=(rows, P(), P(None, "head"), columns, columns),
        out_specs=(columns, columns, columns),
        check_vma=False,
    )
```
